512 devices in a mesh: row: 16 (over x, z_lo), col: 32 (over y, z_hi, core).
Axes of the slice: x: 4, y: 8, z: 8 (z_hi: 2, z_lo: 4; z = z_hi * 4 + z_lo), core: 2. Of those that a mesh axis runs over, the one named last changes fastest.
Arguments:
- covariance: float32 [16384, 16384], P('row', 'col'), may hold values from -7 to 14, as said below
- wind_mask: int32 [2, 16384], replicated, may hold values 0 or 1
- wind_speed: float32 [2, 16384], replicated, may hold values from 0.02 to 0.3
- obs_cells: int32 [256, 128], replicated, may hold values from 0 to 16383
- obs_scale: float32 [256], replicated, may hold values from 0.05 to 0.2
- gain: bfloat16 [16384, 256], P('row'), may hold values from -0.375 to 0.375
Outputs:
- updated: float32 [16384, 16384], P('row', 'col')
The draws below stay inside these ranges and needn't reach their ends.
Inputs may be any that keep to these rules, and one draw needn't show every extreme that they name: A covariance window.
All inputs are finite; a program needn't handle non-finite values.
Results may differ from the reference program's by a relative error of at most 0.0003.
Values sent between devices are 32-bit elements; how exact they have to be, the bound alone decides.
No kernel may reach another device: no remote copies, remote signals or barrier semaphores. Data moves between devices by JAX's collectives and lax.ppermute only.
A program may use at most 64 MiB of HBM per device.

```python
import jax
import jax.numpy as jnp
from jax import lax

MAPX = 256
NOBS = 256
FOOT = 128
W = 16384


def draw_covariance(key, part):
    first_key = jax.random.fold_in(jax.random.fold_in(key, 17), 0)
    matrix = jnp.clip(jax.random.normal(first_key, (W, W), jnp.float32), -4.0, 4.0) * 0.5
    matrix = matrix + 2.0 * jnp.eye(W, dtype=jnp.float32)
    return matrix.astype(jnp.float32)


def plant(array, rng, smallest, largest):
    longest = array.shape.index(max(array.shape))
    spots = []
    for shift in (0, 1):
        where = [jax.random.randint(jax.random.fold_in(rng, axis), (), 0, length) for axis, length in enumerate(array.shape)]
        where[longest] = (where[longest] + shift) % array.shape[longest]
        spots.append(tuple(where))
    return array.at[spots[0]].set(smallest).at[spots[1]].set(largest)


def levels(rng, dims, shards, low, high):
    level = 1.0
    for position, parts in shards:
        steps = jax.random.uniform(jax.random.fold_in(jax.random.fold_in(rng, 6), position), (parts,), jnp.float32, low / len(shards), high / len(shards))
        level = level * jnp.repeat(jnp.exp(steps), dims[position] // parts).reshape((-1,) + (1,) * (len(dims) - 1 - position))
    return level


def normal_values(key, extent, deviation, most, cuts=(), kind=jnp.bfloat16):
    values = jax.random.normal(key, extent, jnp.float32) * deviation
    if len(cuts) > 0:
        values = levels(key, extent, cuts, -0.22, 0.18) * values
    return jnp.clip(values, min=-most, max=most).astype(kind)


def setup_inputs(seed: int = 0) -> dict:
    streams_of = jax.random.split(jax.random.key(seed), 7)
    covariance = draw_covariance(jax.random.fold_in(streams_of[6], 71), 0)
    wind_mask = plant((jax.random.randint(streams_of[1], (2, W), 0, 2) < 1).astype(jnp.int32), jax.random.fold_in(streams_of[1], 1), 0, 1)
    wind_speed = jnp.clip(jax.random.uniform(streams_of[2], (2, W), jnp.float32, 0.02, 0.3), 0.02, 0.3)
    obs_cells = plant(jax.random.randint(streams_of[3], (NOBS, FOOT), 0, W), jax.random.fold_in(streams_of[3], 1), 0, W - 1).astype(jnp.int32)
    obs_scale = jnp.clip(jax.random.uniform(streams_of[4], (NOBS,), jnp.float32, 0.05, 0.2), 0.05, 0.2)
    gain = normal_values(streams_of[5], (W, NOBS), NOBS ** -0.5, 0.375, ((0, 16),))
    return {"covariance": covariance, "wind_mask": wind_mask, "wind_speed": wind_speed, "obs_cells": obs_cells, "obs_scale": obs_scale, "gain": gain}


diffusion = 0.05


def coefficients(wind_mask, wind_speed):
    cell_total = wind_speed.shape[1]
    cells = jnp.arange(cell_total, dtype=jnp.int32)
    map_column = cells % MAPX
    map_row = cells // MAPX
    last_row = cell_total // MAPX - 1
    speed_x = wind_speed[0]
    speed_y = wind_speed[1]
    sign_x = wind_mask[0].astype(jnp.float32)
    sign_y = wind_mask[1].astype(jnp.float32)
    middle = 1.0 - speed_x - speed_y - 4.0 * diffusion
    western = jnp.where(map_column > 0, speed_x * sign_x + diffusion, 0.0)
    eastern = jnp.where(map_column < MAPX - 1, speed_x * (1.0 - sign_x) + diffusion, 0.0)
    northern = jnp.where(map_row > 0, speed_y * sign_y + diffusion, 0.0)
    southern = jnp.where(map_row < last_row, speed_y * (1.0 - sign_y) + diffusion, 0.0)
    return jnp.stack([middle, western, eastern, northern, southern]).astype(jnp.float32)


def transport(extended, coef, along_dim):
    length = extended.shape[along_dim] - 2 * MAPX
    if along_dim == 0:
        weights = coef[:, :, None]
    else:
        weights = coef[:, None, :]

    def window_at(offset):
        return lax.slice_in_dim(extended, offset, offset + length, axis=along_dim)

    result = weights[0] * window_at(MAPX) + weights[1] * window_at(MAPX - 1)
    result = result + weights[2] * window_at(MAPX + 1)
    result = result + weights[3] * window_at(0) + weights[4] * window_at(2 * MAPX)
    return result


def reference(covariance, wind_mask, wind_speed, obs_cells, obs_scale, gain):
    table = coefficients(wind_mask, wind_speed)
    moved_field = covariance
    for repeat in range(2):
        moved_field = transport(jnp.pad(moved_field, ((MAPX, MAPX), (0, 0))), table, 0)
        moved_field = transport(jnp.pad(moved_field, ((0, 0), (MAPX, MAPX))), table, 1)

    def observe(inputs):
        cell_list, weight_one = inputs
        return weight_one * jnp.sum(moved_field[cell_list], axis=0)

    observed = lax.map(observe, (obs_cells, obs_scale))
    update = jnp.dot(gain.astype(jnp.float32), observed, precision=lax.Precision.HIGHEST, preferred_element_type=jnp.float32)
    return moved_field - update
```

```python
import jax
import jax.numpy as jnp
from jax import lax
from jax.sharding import PartitionSpec as P

MAPX = 256


diffusion = 0.05
HIGH = lax.Precision.HIGHEST


def coefficients(wind_mask, wind_speed):
    cell_total = wind_speed.shape[1]
    cells = jnp.arange(cell_total, dtype=jnp.int32)
    map_column = cells % MAPX
    map_row = cells // MAPX
    last_row = cell_total // MAPX - 1
    speed_x = wind_speed[0]
    speed_y = wind_speed[1]
    sign_x = wind_mask[0].astype(jnp.float32)
    sign_y = wind_mask[1].astype(jnp.float32)
    middle = 1.0 - speed_x - speed_y - 4.0 * diffusion
    western = jnp.where(map_column > 0, speed_x * sign_x + diffusion, 0.0)
    eastern = jnp.where(map_column < MAPX - 1, speed_x * (1.0 - sign_x) + diffusion, 0.0)
    northern = jnp.where(map_row > 0, speed_y * sign_y + diffusion, 0.0)
    southern = jnp.where(map_row < last_row, speed_y * (1.0 - sign_y) + diffusion, 0.0)
    return jnp.stack([middle, western, eastern, northern, southern])


def after(value, *earlier):
    return lax.optimization_barrier((value,) + earlier)[0]


def along(array, start, size, dim):
    return lax.slice_in_dim(array, start, start + size, axis=dim)


def transport(extended, weights, dim):
    length = extended.shape[dim] - 2 * MAPX
    shape = (5, length, 1) if dim == 0 else (5, 1, length)
    weights = weights.reshape(shape)
    result = weights[0] * along(extended, MAPX, length, dim)
    result = result + weights[1] * along(extended, MAPX - 1, length, dim)
    result = result + weights[2] * along(extended, MAPX + 1, length, dim)
    result = result + weights[3] * along(extended, 0, length, dim)
    return result + weights[4] * along(extended, 2 * MAPX, length, dim)


def transposed(select, weights):
    length = select.shape[1] - 2 * MAPX

    def term(k, offset):
        return along(weights, offset, length, 1)[k] * along(select, offset, length, 1)

    result = term(0, MAPX) + term(1, MAPX + 1) + term(2, MAPX - 1)
    return result + term(3, 2 * MAPX) + term(4, 0)


def local(covariance, wind_mask, wind_speed, obs_cells, obs_scale, gain):
    rows, cols = covariance.shape
    reach = 2 * MAPX
    row_parts = lax.axis_size("row")
    col_parts = lax.axis_size("col")
    row_at = lax.axis_index("row")
    col_at = lax.axis_index("col")
    down = [(i, i + 1) for i in range(row_parts - 1)]
    up = [(i + 1, i) for i in range(row_parts - 1)]
    east = [(j, j + 1) for j in range(col_parts - 1)]
    west = [(j + 1, j) for j in range(col_parts - 1)]

    groups = [along(covariance, MAPX * g, MAPX, 0) for g in range(rows // MAPX)]

    def swap_cols(block):
        return lax.ppermute(block, "col", east), lax.ppermute(block, "col", west)

    table = coefficients(wind_mask, wind_speed)
    table = jnp.pad(table, ((0, 0), (reach, reach)))
    row_weights = lax.dynamic_slice_in_dim(table, row_at * rows, rows + 2 * reach, 1)
    col_weights = lax.dynamic_slice_in_dim(table, col_at * cols + MAPX, cols + 2 * MAPX, 1)

    def move_cols(block, west_side, east_side):
        extended = jnp.concatenate([west_side, block, east_side], axis=1)
        once = transport(extended, col_weights, 1)
        return transport(once, along(col_weights, MAPX, cols, 1), 1)

    order = (0, 3, 1, 2)
    sides = {}
    moved = {}
    halo = {}
    for n in (0, 3):
        sides[n] = swap_cols(groups[n])
    for k, n in enumerate(order):
        moved[n] = move_cols(groups[n], *sides[n])
        halo[n] = lax.ppermute(moved[n], "row", up if n < 2 else down)
        if k < 2:
            later = order[k + 2]
            sides[later] = swap_cols(after(groups[later], moved[n]))

    window = rows + 2 * reach
    obs_count, foot = obs_cells.shape
    lane = 128
    place = obs_cells - (row_at * rows - reach)
    block_hit = (place[:, None, :] >> 7) == jnp.arange(window // lane, dtype=jnp.int32)[None, :, None]
    lane_hit = (place[:, :, None] & (lane - 1)) == jnp.arange(lane, dtype=jnp.int32)[None, None, :]
    counts = jnp.einsum(
        "obm,oml->obl",
        block_hit.astype(jnp.bfloat16),
        lane_hit.astype(jnp.bfloat16),
        preferred_element_type=jnp.float32,
    ).reshape(obs_count, window)
    select = counts * obs_scale[:, None]
    select = transposed(select, row_weights)
    select = transposed(select, along(row_weights, MAPX, rows + 2 * MAPX, 1))
    part = jnp.dot(select, covariance, precision=HIGH, preferred_element_type=jnp.float32)

    outer = inner = 4
    assert row_parts == outer * inner
    x_at = row_at // inner
    z_at = row_at % inner

    def shift_x(d):
        return [(i, (i // inner + d) % outer * inner + i % inner) for i in range(row_parts)]

    def shift_z(d):
        return [(i, i // inner * inner + (i + d) % inner) for i in range(row_parts)]

    def scatter_sum(value, at, count, shift):
        size = value.shape[0] // count
        total = lax.dynamic_slice_in_dim(value, at * size, size, 0)
        for d in range(1, count):
            piece = lax.dynamic_slice_in_dim(value, (at + d) % count * size, size, 0)
            total = total + lax.ppermute(piece, "row", shift(d))
        return total

    def gather(value, at, count, shift):
        size = value.shape[0]
        result = jnp.zeros((count * size,) + value.shape[1:], value.dtype)
        result = lax.dynamic_update_slice_in_dim(result, value, at * size, 0)
        for d in range(1, count):
            piece = lax.ppermute(value, "row", shift(d))
            result = lax.dynamic_update_slice_in_dim(result, piece, (at - d) % count * size, 0)
        return result

    piece = scatter_sum(part, x_at, outer, shift_x)
    piece = scatter_sum(piece, z_at, inner, shift_z)
    piece = move_cols(piece, *swap_cols(piece))
    observed = gather(piece, z_at, inner, shift_z)
    observed = gather(observed, x_at, outer, shift_x)
    update = jnp.dot(
        gain.astype(jnp.float32), observed, precision=HIGH, preferred_element_type=jnp.float32
    )

    extended = jnp.concatenate(
        [jnp.zeros_like(halo[2]), halo[3], moved[0], moved[1], moved[2], moved[3], halo[0], halo[1]]
    )
    once = transport(extended, along(row_weights, MAPX, rows + 2 * MAPX, 1), 0)
    result = transport(once, along(row_weights, reach, rows, 1), 0) - update
    far = along(row_weights, reach, MAPX, 1)[3] * along(row_weights, MAPX, MAPX, 1)[3]
    last = result[:MAPX] + far[:, None] * halo[2]
    return lax.dynamic_update_slice_in_dim(result, last, 0, 0)


def solution(mesh):
    placed = (P("row", "col"), P(), P(), P(), P(), P("row", None))
    return jax.shard_map(
        local, mesh=mesh, in_specs=placed, out_specs=P("row", "col"), check_vma=False
    )
```

```python
import jax
import jax.numpy as jnp
from jax import lax
from jax.experimental import pallas as pl
from jax.experimental.pallas import tpu as pltpu
from jax.sharding import PartitionSpec as P


MAPX = 256


diffusion = 0.05
HIGH = lax.Precision.HIGHEST


def coefficients(wind_mask, wind_speed):
    cell_total = wind_speed.shape[1]
    cells = jnp.arange(cell_total, dtype=jnp.int32)
    map_column = cells % MAPX
    map_row = cells // MAPX
    last_row = cell_total // MAPX - 1
    speed_x = wind_speed[0]
    speed_y = wind_speed[1]
    sign_x = wind_mask[0].astype(jnp.float32)
    sign_y = wind_mask[1].astype(jnp.float32)
    middle = 1.0 - speed_x - speed_y - 4.0 * diffusion
    western = jnp.where(map_column > 0, speed_x * sign_x + diffusion, 0.0)
    eastern = jnp.where(map_column < MAPX - 1, speed_x * (1.0 - sign_x) + diffusion, 0.0)
    northern = jnp.where(map_row > 0, speed_y * sign_y + diffusion, 0.0)
    southern = jnp.where(map_row < last_row, speed_y * (1.0 - sign_y) + diffusion, 0.0)
    return jnp.stack([middle, western, eastern, northern, southern])


def after(value, *earlier):
    return lax.optimization_barrier((value,) + earlier)[0]


def along(array, start, size, dim):
    return lax.slice_in_dim(array, start, start + size, axis=dim)


def transposed(select, weights):
    length = select.shape[1] - 2 * MAPX

    def term(k, offset):
        return along(weights, offset, length, 1)[k] * along(select, offset, length, 1)

    result = term(0, MAPX) + term(1, MAPX + 1) + term(2, MAPX - 1)
    return result + term(3, 2 * MAPX) + term(4, 0)


def step_cols(before, here, behind, weights):
    width = here.shape[1]
    result = weights[0] * here + weights[1] * pltpu.roll(here, 1, 1)
    result = result + weights[2] * pltpu.roll(here, width - 1, 1)
    return result + weights[3] * before + weights[4] * behind


def cols_kernel(core_ref, here_ref, near_ref, far_ref, weights_ref, out_ref):
    first = core_ref[0] == 0
    near, far = near_ref[...], far_ref[...]
    west = jnp.where(first, far, near)
    east = jnp.where(first, near, far)
    here = here_ref[...]
    maps = [piece[:, MAPX * k : MAPX * (k + 1)] for piece in (west, here, east) for k in range(2)]

    def weights(m):
        return [weights_ref[k : k + 1, MAPX * m : MAPX * (m + 1)] for k in range(5)]

    once = [step_cols(maps[m], maps[m + 1], maps[m + 2], weights(m)) for m in range(4)]
    for m in range(2):
        out_ref[:, MAPX * m : MAPX * (m + 1)] = step_cols(
            once[m], once[m + 1], once[m + 2], weights(m + 1)
        )


def move_cols(core, here, here_at, near, near_at, far, weights, rows):
    cols = here.shape[1]
    tile = min(rows, 32)
    steps = rows // tile
    return pl.pallas_call(
        cols_kernel,
        out_shape=jax.ShapeDtypeStruct((rows, cols), jnp.float32),
        grid_spec=pltpu.PrefetchScalarGridSpec(
            num_scalar_prefetch=1,
            grid=(steps,),
            in_specs=[
                pl.BlockSpec((tile, cols), lambda s, c: (here_at * steps + s, 0)),
                pl.BlockSpec((tile, cols), lambda s, c: (near_at * steps + s, 0)),
                pl.BlockSpec((tile, cols), lambda s, c: (s, 0)),
                pl.BlockSpec(weights.shape, lambda s, c: (0, 0)),
            ],
            out_specs=pl.BlockSpec((tile, cols), lambda s, c: (s, 0)),
        ),
        cost_estimate=pl.CostEstimate(
            flops=27 * rows * cols, bytes_accessed=16 * rows * cols, transcendentals=0
        ),
        name="move_cols",
    )(core, here, near, far, weights)


def step_rows(before, here, behind, weights):
    height = here.shape[0]
    result = weights[:, 0:1] * here + weights[:, 1:2] * pltpu.roll(here, 1, 0)
    result = result + weights[:, 2:3] * pltpu.roll(here, height - 1, 0)
    if before is not None:
        result = result + weights[:, 3:4] * before
    return result + weights[:, 4:5] * behind


def rows_kernel(*refs):
    maps, update_ref, weights_ref, out_ref, once_ref = refs[:7], *refs[7:]
    for m in range(6):
        once_ref[MAPX * m : MAPX * (m + 1)] = step_rows(
            maps[m - 1][...] if m > 0 else None,
            maps[m][...],
            maps[m + 1][...],
            weights_ref[MAPX * m : MAPX * (m + 1)],
        )
    for m in range(1, 5):
        out_ref[MAPX * (m - 1) : MAPX * m] = (
            step_rows(
                once_ref[MAPX * (m - 1) : MAPX * m],
                once_ref[MAPX * m : MAPX * (m + 1)],
                once_ref[MAPX * (m + 1) : MAPX * (m + 2)],
                weights_ref[MAPX * m : MAPX * (m + 1)],
            )
            - update_ref[MAPX * (m - 1) : MAPX * m]
        )


def move_rows(maps, update, weights):
    rows, cols = update.shape
    tile = 128
    one = pl.BlockSpec((MAPX, tile), lambda s: (0, s))
    whole = pl.BlockSpec((rows, tile), lambda s: (0, s))
    return pl.pallas_call(
        rows_kernel,
        out_shape=jax.ShapeDtypeStruct((rows, cols), jnp.float32),
        grid=(cols // tile,),
        in_specs=[one] * 7 + [whole, pl.BlockSpec(weights.shape, lambda s: (0, 0))],
        out_specs=whole,
        scratch_shapes=[pltpu.VMEM((rows + 2 * MAPX, tile), jnp.float32)],
        cost_estimate=pl.CostEstimate(
            flops=24 * rows * cols, bytes_accessed=16 * rows * cols, transcendentals=0
        ),
        name="move_rows",
    )(*maps, update, weights)


def last_kernel(result_ref, halo_ref, weights_ref, before_ref, out_ref):
    factor = weights_ref[:, 3:4] * before_ref[:, 3:4]
    out_ref[...] = result_ref[...] + factor * halo_ref[...]


def add_last(result, halo, weights):
    cols = result.shape[1]
    tile = 128
    steps = MAPX // tile
    block = pl.BlockSpec((tile, cols), lambda s: (s, 0))
    return pl.pallas_call(
        last_kernel,
        out_shape=jax.ShapeDtypeStruct(result.shape, result.dtype),
        grid=(steps,),
        in_specs=[
            block,
            block,
            pl.BlockSpec((tile, weights.shape[1]), lambda s: (steps + s, 0)),
            pl.BlockSpec((tile, weights.shape[1]), lambda s: (s, 0)),
        ],
        out_specs=block,
        input_output_aliases={0: 0},
        cost_estimate=pl.CostEstimate(
            flops=2 * MAPX * cols, bytes_accessed=12 * MAPX * cols, transcendentals=0
        ),
        name="add_last",
    )(result, halo, weights, weights)


def local(covariance, wind_mask, wind_speed, obs_cells, obs_scale, gain):
    rows, cols = covariance.shape
    reach = 2 * MAPX
    row_parts = lax.axis_size("row")
    col_parts = lax.axis_size("col")
    row_at = lax.axis_index("row")
    col_at = lax.axis_index("col")
    down = [(i, i + 1) for i in range(row_parts - 1)]
    up = [(i + 1, i) for i in range(row_parts - 1)]
    near_swap = [(j, j ^ 1) for j in range(col_parts)]
    far_swap = [(j, (j - 1 ^ 1) + 1) for j in range(1, col_parts - 1)]
    core = (col_at % 2).reshape(1)

    def group(n):
        return along(covariance, MAPX * n, MAPX, 0)

    far = {n: lax.ppermute(group(n), "col", far_swap) for n in (0, 3)}
    near = lax.ppermute(covariance, "col", near_swap)

    table = coefficients(wind_mask, wind_speed)
    table = jnp.pad(table, ((0, 0), (reach, reach)))
    row_weights = lax.dynamic_slice_in_dim(table, row_at * rows, rows + 2 * reach, 1)
    col_weights = lax.dynamic_slice_in_dim(table, col_at * cols + MAPX, cols + 2 * MAPX, 1)
    down_weights = along(row_weights, MAPX, rows + 2 * MAPX, 1).T

    pieces = row_parts
    obs_count, foot = obs_cells.shape
    each = obs_count // pieces
    order = jnp.arange(pieces, dtype=jnp.int32) ^ row_at
    cells = obs_cells.reshape(pieces, each, foot)[order].reshape(obs_count, foot)
    scale = obs_scale.reshape(pieces, each)[order].reshape(obs_count)
    window = rows + 2 * reach
    lane = 128
    place = cells - (row_at * rows - reach)
    block_hit = (place[:, None, :] >> 7) == jnp.arange(window // lane, dtype=jnp.int32)[None, :, None]
    lane_hit = (place[:, :, None] & (lane - 1)) == jnp.arange(lane, dtype=jnp.int32)[None, None, :]
    counts = jnp.einsum(
        "obm,oml->obl",
        block_hit.astype(jnp.bfloat16),
        lane_hit.astype(jnp.bfloat16),
        preferred_element_type=jnp.float32,
    ).reshape(obs_count, window)
    select = transposed(counts * scale[:, None], row_weights)
    select = transposed(select, along(row_weights, MAPX, rows + 2 * MAPX, 1))
    part = jnp.dot(select, covariance, precision=HIGH, preferred_element_type=jnp.float32)

    def move_group(n, *earlier):
        return move_cols(core, covariance, n, near, n, after(far[n], *earlier), col_weights, MAPX)

    def across(bit):
        return [(i, i ^ bit) for i in range(row_parts)]

    bits = [8, 4, 2, 1]
    assert row_parts == 16

    moved, halo = {}, {}
    moved[0] = move_group(0, part)
    halo[0] = lax.ppermute(moved[0], "row", up)
    far[1] = lax.ppermute(after(group(1), moved[0]), "col", far_swap)

    total = after(part, moved[0])
    for bit in bits:
        half = total.shape[0] // 2
        total = total[:half] + lax.ppermute(total[half:], "row", across(bit))

    moved[3] = move_group(3, total)
    halo[3] = lax.ppermute(moved[3], "row", down)
    far[2] = lax.ppermute(after(group(2), moved[3]), "col", far_swap)

    total = after(total, moved[3])
    piece_far = lax.ppermute(total, "col", far_swap)
    piece_near = lax.ppermute(total, "col", near_swap)
    observed = move_cols(core, total, 0, piece_near, 0, piece_far, col_weights, each)
    for bit in bits[:1:-1]:
        observed = jnp.concatenate([observed, lax.ppermute(observed, "row", across(bit))])

    moved[1] = move_group(1, observed)
    halo[1] = lax.ppermute(moved[1], "row", up)

    observed = after(observed, moved[1])
    for bit in bits[1::-1]:
        observed = jnp.concatenate([observed, lax.ppermute(observed, "row", across(bit))])
    index = jnp.arange(obs_count, dtype=jnp.int32)
    reorder = (index[:, None] ^ (row_at * each)) == index[None, :]
    ordered_gain = jnp.dot(gain, reorder.astype(gain.dtype), preferred_element_type=jnp.float32)
    update = jnp.dot(ordered_gain, observed, precision=HIGH, preferred_element_type=jnp.float32)

    moved[2] = move_group(2, update)
    halo[2] = lax.ppermute(moved[2], "row", down)

    maps = [halo[3], moved[0], moved[1], moved[2], moved[3], halo[0], halo[1]]
    result = move_rows(maps, update, down_weights)
    return add_last(result, halo[2], down_weights)


def solution(mesh):
    placed = (P("row", "col"), P(), P(), P(), P(), P("row", None))
    return jax.shard_map(
        local, mesh=mesh, in_specs=placed, out_specs=P("row", "col"), check_vma=False
    )
```

```python
import jax
import jax.numpy as jnp
from jax import lax
from jax.experimental import pallas as pl
from jax.experimental.pallas import tpu as pltpu
from jax.sharding import PartitionSpec as P


MAPX = 256
LANE = 128


diffusion = 0.05
HIGH = lax.Precision.HIGHEST
SMALL = pltpu.CompilerParams(vmem_limit_bytes=16 << 20)


def after(value, *earlier):
    return lax.optimization_barrier((value,) + earlier)[0]


def along(array, start, size, dim):
    return lax.slice_in_dim(array, start, start + size, axis=dim)


def weights_kernel(map_total, ahead, at_ref, mask_ref, speed_ref, rows_ref, cols_ref, down_ref):
    for ref, number in ((rows_ref, 0), (cols_ref, 1)):
        for m in range(ref.shape[1] // MAPX):
            map_row = at_ref[number] + m - ahead[number]
            inside = (map_row >= 0) & (map_row < map_total)
            cells = pl.ds(pl.multiple_of(jnp.clip(map_row, 0, map_total - 1) * MAPX, MAPX), MAPX)
            speed = speed_ref[:, cells]
            sign = mask_ref[:, cells].astype(jnp.float32)
            column = lax.broadcasted_iota(jnp.int32, (1, MAPX), 1)
            speed_x, speed_y = speed[0:1], speed[1:2]
            sign_x, sign_y = sign[0:1], sign[1:2]
            middle = 1.0 - speed_x - speed_y - 4.0 * diffusion
            western = jnp.where(column > 0, speed_x * sign_x + diffusion, 0.0)
            eastern = jnp.where(column < MAPX - 1, speed_x * (1.0 - sign_x) + diffusion, 0.0)
            northern = jnp.where(map_row > 0, speed_y * sign_y + diffusion, 0.0)
            southern = jnp.where(map_row < map_total - 1, speed_y * (1.0 - sign_y) + diffusion, 0.0)
            zero = jnp.zeros_like(middle)
            table = jnp.concatenate(
                [middle, western, eastern, northern, southern, zero, zero, zero], axis=0
            )
            table = jnp.where(inside, table, 0.0)
            ref[:, MAPX * m : MAPX * (m + 1)] = table
            if number == 0 and 0 < m < ref.shape[1] // MAPX - 1:
                down_ref[MAPX * (m - 1) : MAPX * m, :] = table.T


def local_weights(at, wind_mask, wind_speed, rows, cols):
    map_total = wind_speed.shape[1] // MAPX

    def kernel(*refs):
        weights_kernel(map_total, (2, 1), *refs)

    return pl.pallas_call(
        kernel,
        out_shape=(
            jax.ShapeDtypeStruct((8, rows + 4 * MAPX), jnp.float32),
            jax.ShapeDtypeStruct((8, cols + 2 * MAPX), jnp.float32),
            jax.ShapeDtypeStruct((rows + 2 * MAPX, 8), jnp.float32),
        ),
        grid_spec=pltpu.PrefetchScalarGridSpec(
            num_scalar_prefetch=1,
            grid=(1,),
            in_specs=[pl.BlockSpec(wind_mask.shape, lambda s, a: (0, 0))] * 2,
            out_specs=(
                pl.BlockSpec((8, rows + 4 * MAPX), lambda s, a: (0, 0)),
                pl.BlockSpec((8, cols + 2 * MAPX), lambda s, a: (0, 0)),
                pl.BlockSpec((rows + 2 * MAPX, 8), lambda s, a: (0, 0)),
            ),
        ),
        compiler_params=SMALL,
        cost_estimate=pl.CostEstimate(flops=1 << 16, bytes_accessed=1 << 20, transcendentals=0),
        name="local_weights",
    )(at, wind_mask, wind_speed)


def select_kernel(rows, at_ref, cells_ref, scale_ref, weights_ref, out_ref, counts_ref):
    each = cells_ref.shape[0]
    window = weights_ref.shape[1]
    blocks = window // LANE
    place = cells_ref[...] - (at_ref[0] * rows - 2 * MAPX)
    block_of, lane_of = place >> 7, place & (LANE - 1)
    block_index = lax.broadcasted_iota(jnp.int32, (blocks, LANE), 0)
    lane_index = lax.broadcasted_iota(jnp.int32, (LANE, LANE), 0)
    for o in range(each):
        block_hit = jnp.where(block_of[o : o + 1] == block_index, 1.0, 0.0).astype(jnp.bfloat16)
        lane_hit = jnp.where(lane_of[o : o + 1] == lane_index, 1.0, 0.0).astype(jnp.bfloat16)
        counts_ref[o] = lax.dot_general(
            block_hit, lane_hit, (((1,), (1,)), ((), ())), preferred_element_type=jnp.float32
        )
    scale = scale_ref[...]

    def weights(k, m):
        return weights_ref[k : k + 1, MAPX * m : MAPX * (m + 1)]

    maps = [
        scale * jnp.concatenate([counts_ref[:, 2 * m, :], counts_ref[:, 2 * m + 1, :]], axis=1)
        for m in range(window // MAPX)
    ]
    for first in (1, 2):
        moved = []
        for m in range(1, len(maps) - 1):
            t = m + first - 1
            here = maps[m]
            value = weights(0, t) * here + pltpu.roll(weights(1, t) * here, MAPX - 1, 1)
            value = value + pltpu.roll(weights(2, t) * here, 1, 1)
            value = value + weights(3, t + 1) * maps[m + 1] + weights(4, t - 1) * maps[m - 1]
            moved.append(value)
        maps = moved
    for m, value in enumerate(maps):
        out_ref[:, MAPX * m : MAPX * (m + 1)] = value


def observation_rows(at, obs_cells, obs_scale, weights, rows, pieces):
    obs_count, foot = obs_cells.shape
    each = obs_count // pieces

    def kernel(*refs):
        select_kernel(rows, *refs)

    return pl.pallas_call(
        kernel,
        out_shape=jax.ShapeDtypeStruct((obs_count, rows), jnp.float32),
        grid_spec=pltpu.PrefetchScalarGridSpec(
            num_scalar_prefetch=1,
            grid=(pieces,),
            in_specs=[
                pl.BlockSpec((each, foot), lambda s, a: (s ^ a[2], 0)),
                pl.BlockSpec((each, 1), lambda s, a: (s ^ a[2], 0)),
                pl.BlockSpec(weights.shape, lambda s, a: (0, 0)),
            ],
            out_specs=pl.BlockSpec((each, rows), lambda s, a: (s, 0)),
            scratch_shapes=[pltpu.VMEM((each, weights.shape[1] // LANE, LANE), jnp.float32)],
        ),
        compiler_params=SMALL,
        cost_estimate=pl.CostEstimate(flops=1 << 27, bytes_accessed=1 << 21, transcendentals=0),
        name="observation_rows",
    )(at[2:], obs_cells, obs_scale[:, None], weights)


def step_cols(before, here, behind, weights):
    width = here.shape[1]
    result = weights[0] * here + weights[1] * pltpu.roll(here, 1, 1)
    result = result + weights[2] * pltpu.roll(here, width - 1, 1)
    return result + weights[3] * before + weights[4] * behind


def cols_kernel(inner, unroll, core_ref, here_ref, near_ref, *refs):
    far_refs, (weights_ref, out_ref) = refs[:-2], refs[-2:]
    first = core_ref[0] == 0

    def weights(m):
        return [weights_ref[k : k + 1, MAPX * m : MAPX * (m + 1)] for k in range(5)]

    def body(t, carry):
        rows = pl.ds(pl.multiple_of(t * inner, inner), inner)
        near, here = near_ref[rows, :], here_ref[rows, :]
        far = far_refs[0][rows, :]
        for ref in far_refs[1:]:
            far = far + ref[rows, :]
        west = jnp.where(first, far, near)
        east = jnp.where(first, near, far)
        maps = [part[:, MAPX * k : MAPX * (k + 1)] for part in (west, here, east) for k in range(2)]
        once = [step_cols(maps[m], maps[m + 1], maps[m + 2], weights(m)) for m in range(4)]
        for m in range(2):
            out_ref[rows, MAPX * m : MAPX * (m + 1)] = step_cols(
                once[m], once[m + 1], once[m + 2], weights(m + 1)
            )
        return carry

    lax.fori_loop(0, here_ref.shape[0] // inner, body, 0, unroll=unroll)


def move_cols(core, here, near, fars, weights, rows):
    cols = here[0].shape[1]
    tile = min(rows, 128)
    inner = min(rows, 64)
    steps = rows // tile

    def kernel(*refs):
        cols_kernel(inner, tile // inner, *refs)

    def spec(at):
        return pl.BlockSpec((tile, cols), lambda s, c: (at * steps + s, 0))

    blocks = [here, near, *fars]
    return pl.pallas_call(
        kernel,
        out_shape=jax.ShapeDtypeStruct((rows, cols), jnp.float32),
        grid_spec=pltpu.PrefetchScalarGridSpec(
            num_scalar_prefetch=1,
            grid=(steps,),
            in_specs=[spec(at) for _, at in blocks]
            + [pl.BlockSpec(weights.shape, lambda s, c: (0, 0))],
            out_specs=spec(0),
        ),
        compiler_params=SMALL,
        cost_estimate=pl.CostEstimate(
            flops=27 * rows * cols, bytes_accessed=16 * rows * cols, transcendentals=0
        ),
        name="move_cols",
    )(core, *[array for array, _ in blocks], weights)


def rows_kernel(chunk, *refs):
    maps, (update_ref, weights_ref, out_ref, once_ref) = refs[:7], refs[7:]

    def step(source, base, before, behind, weights_at, emit):
        def body(c, carry):
            start = pl.multiple_of(c * chunk, chunk)
            low = pl.multiple_of(jnp.maximum(start - 8, 0), 8)
            high = pl.multiple_of(jnp.minimum(start + chunk, MAPX - 8), 8)
            here = source[pl.ds(base + start, chunk), :]
            wide = jnp.concatenate(
                [source[pl.ds(base + low, 8), :], here, source[pl.ds(base + high, 8), :]], axis=0
            )
            weights = weights_ref[pl.ds(weights_at + start, chunk), :]
            value = weights[:, 0:1] * here
            value = value + weights[:, 1:2] * pltpu.roll(wide, 1, 0)[8 : 8 + chunk]
            value = value + weights[:, 2:3] * pltpu.roll(wide, chunk + 15, 0)[8 : 8 + chunk]
            if before is not None:
                value = value + weights[:, 3:4] * before[0][pl.ds(before[1] + start, chunk), :]
            value = value + weights[:, 4:5] * behind[0][pl.ds(behind[1] + start, chunk), :]
            emit(start, value)
            return carry

        lax.fori_loop(0, MAPX // chunk, body, 0, unroll=MAPX // chunk)

    for m in range(6):

        def emit(start, value, m=m):
            once_ref[pl.ds(MAPX * m + start, chunk), :] = value

        step(maps[m], 0, (maps[m - 1], 0) if m > 0 else None, (maps[m + 1], 0), MAPX * m, emit)
    for m in range(1, 5):

        def emit(start, value, m=m):
            rows = pl.ds(MAPX * (m - 1) + start, chunk)
            out_ref[rows, :] = value - update_ref[rows, :]

        step(
            once_ref, MAPX * m, (once_ref, MAPX * (m - 1)), (once_ref, MAPX * (m + 1)), MAPX * m, emit
        )


def move_rows(maps, update, weights):
    rows, cols = update.shape

    def kernel(*refs):
        rows_kernel(64, *refs)

    def whole(array):
        return pl.BlockSpec(array.shape, lambda s: (0, 0))

    return pl.pallas_call(
        kernel,
        out_shape=jax.ShapeDtypeStruct((rows, cols), jnp.float32),
        grid=(1,),
        in_specs=[whole(array) for array in (*maps, update, weights)],
        out_specs=whole(update),
        scratch_shapes=[pltpu.VMEM((rows + 2 * MAPX, cols), jnp.float32)],
        compiler_params=SMALL,
        cost_estimate=pl.CostEstimate(
            flops=24 * rows * cols, bytes_accessed=16 * rows * cols, transcendentals=0
        ),
        name="move_rows",
    )(*maps, update, weights)


def last_kernel(result_ref, halo_ref, weights_ref, before_ref, out_ref):
    factor = weights_ref[:, 3:4] * before_ref[:, 3:4]
    out_ref[...] = result_ref[...] + factor * halo_ref[...]


def add_last(result, halo, weights):
    cols = result.shape[1]
    tile = 128
    steps = MAPX // tile
    block = pl.BlockSpec((tile, cols), lambda s: (s, 0))
    return pl.pallas_call(
        last_kernel,
        out_shape=jax.ShapeDtypeStruct(result.shape, result.dtype),
        grid=(steps,),
        in_specs=[
            block,
            block,
            pl.BlockSpec((tile, weights.shape[1]), lambda s: (steps + s, 0)),
            pl.BlockSpec((tile, weights.shape[1]), lambda s: (s, 0)),
        ],
        out_specs=block,
        input_output_aliases={0: 0},
        compiler_params=SMALL,
        cost_estimate=pl.CostEstimate(
            flops=2 * MAPX * cols, bytes_accessed=12 * MAPX * cols, transcendentals=0
        ),
        name="add_last",
    )(result, halo, weights, weights)


def local(covariance, wind_mask, wind_speed, obs_cells, obs_scale, gain):
    rows, cols = covariance.shape
    row_parts = lax.axis_size("row")
    col_parts = lax.axis_size("col")
    assert row_parts == 16 and rows == 4 * MAPX and cols == 2 * MAPX
    row_at = lax.axis_index("row")
    col_at = lax.axis_index("col")
    down = [(i, i + 1) for i in range(row_parts - 1)]
    up = [(i + 1, i) for i in range(row_parts - 1)]
    near_swap = [(j, j ^ 1) for j in range(col_parts)]
    far_swap = [(j, (j - 1 ^ 1) + 1) for j in range(1, col_parts - 1)]
    turning = [(a, b) for a, b in far_swap if a % 4 in (0, 3)]
    straight = [(a, b) for a, b in far_swap if a % 4 in (1, 2)]
    core = (col_at % 2).reshape(1)
    at = jnp.stack([row_at * (rows // MAPX), col_at * (cols // MAPX), row_at])

    def across(bit):
        return [(i, i ^ bit) for i in range(row_parts)]

    far_turning = lax.ppermute(covariance, "col", turning)
    near = lax.ppermute(covariance, "col", near_swap)

    row_weights, col_weights, down_weights = local_weights(at, wind_mask, wind_speed, rows, cols)
    select = observation_rows(at, obs_cells, obs_scale, row_weights, rows, row_parts)
    part = jnp.dot(select, covariance, precision=HIGH, preferred_element_type=jnp.float32)

    total = part
    for bit in (8, 4):
        half = total.shape[0] // 2
        total = total[:half] + lax.ppermute(total[half:], "row", across(bit))
    each = total.shape[0] // 4
    total = total[:each] + sum(
        lax.ppermute(total[each * bit : each * (bit + 1)], "row", across(bit))
        for bit in (1, 2, 3)
    )

    piece_far = lax.ppermute(total, "col", far_swap)
    order = (0, 3, 1, 2)
    late = after(covariance, select)
    far_straight = {n: lax.ppermute(along(late, MAPX * n, MAPX, 0), "col", straight) for n in order}
    piece_near = lax.ppermute(total, "col", near_swap)
    piece = move_cols(core, (total, 0), (piece_near, 0), [(piece_far, 0)], col_weights, each)
    gathered = [lax.ppermute(piece, "row", across(bit)) for bit in (1, 2, 3)]

    moved, halo = {}, {}
    for n in order:
        moved[n] = move_cols(
            core,
            (covariance, n),
            (near, n),
            [(far_turning, n), (far_straight[n], 0)],
            col_weights,
            MAPX,
        )
        halo[n] = lax.ppermute(moved[n], "row", up if n < 2 else down)

    observed = jnp.concatenate([after(piece, moved[2]), *gathered])
    for bit in (4, 8):
        observed = jnp.concatenate([observed, lax.ppermute(observed, "row", across(bit))])
    index = jnp.arange(gain.shape[1], dtype=jnp.int32)
    reorder = (index[:, None] ^ (row_at * each)) == index[None, :]
    ordered_gain = jnp.dot(gain, reorder.astype(gain.dtype), preferred_element_type=jnp.float32)
    update = jnp.dot(ordered_gain, observed, precision=HIGH, preferred_element_type=jnp.float32)

    maps = [halo[3], moved[0], moved[1], moved[2], moved[3], halo[0], halo[1]]
    result = move_rows(maps, update, down_weights)
    return add_last(result, halo[2], down_weights)


def solution(mesh):
    placed = (P("row", "col"), P(), P(), P(), P(), P("row", None))
    return jax.shard_map(
        local, mesh=mesh, in_specs=placed, out_specs=P("row", "col"), check_vma=False
    )
```

```python
import jax
import jax.numpy as jnp
from jax import lax
from jax.experimental import pallas as pl
from jax.experimental.pallas import tpu as pltpu
from jax.sharding import PartitionSpec as P


MAPX = 256
LANE = 128


diffusion = 0.05
HIGH = lax.Precision.HIGHEST
SMALL = pltpu.CompilerParams(vmem_limit_bytes=16 << 20)


def after(value, *earlier):
    return lax.optimization_barrier((value,) + earlier)[0]


def along(array, start, size, dim):
    return lax.slice_in_dim(array, start, start + size, axis=dim)


def weights_table(map_total, map_row, mask_ref, speed_ref):
    inside = (map_row >= 0) & (map_row < map_total)
    cells = pl.ds(pl.multiple_of(jnp.clip(map_row, 0, map_total - 1) * MAPX, MAPX), MAPX)
    speed = speed_ref[:, cells]
    sign = mask_ref[:, cells].astype(jnp.float32)
    column = lax.broadcasted_iota(jnp.int32, (1, MAPX), 1)
    speed_x, speed_y = speed[0:1], speed[1:2]
    sign_x, sign_y = sign[0:1], sign[1:2]
    middle = 1.0 - speed_x - speed_y - 4.0 * diffusion
    western = jnp.where(column > 0, speed_x * sign_x + diffusion, 0.0)
    eastern = jnp.where(column < MAPX - 1, speed_x * (1.0 - sign_x) + diffusion, 0.0)
    northern = jnp.where(map_row > 0, speed_y * sign_y + diffusion, 0.0)
    southern = jnp.where(map_row < map_total - 1, speed_y * (1.0 - sign_y) + diffusion, 0.0)
    zero = jnp.zeros_like(middle)
    table = jnp.concatenate(
        [middle, western, eastern, northern, southern, zero, zero, zero], axis=0
    )
    return jnp.where(inside, table, 0.0)


def prepare_kernel(rows, map_total, at_ref, mask_ref, speed_ref, *refs):
    cell_refs, (out_ref, cols_ref, down_ref, rows_ref, counts_ref) = refs[:-5], refs[-5:]

    @pl.when(pl.program_id(0) == 0)
    def _():
        last = rows_ref.shape[1] // MAPX - 1
        for m in range(last + 1):
            table = weights_table(map_total, at_ref[0] + m - 2, mask_ref, speed_ref)
            rows_ref[:, MAPX * m : MAPX * (m + 1)] = table
            if 0 < m < last:
                down_ref[MAPX * (m - 1) : MAPX * m, :] = table.T
        for m in range(cols_ref.shape[1] // MAPX):
            cols_ref[:, MAPX * m : MAPX * (m + 1)] = weights_table(
                map_total, at_ref[1] + m - 1, mask_ref, speed_ref
            )

    each = cell_refs[0].shape[0]
    window = rows_ref.shape[1]
    blocks = window // LANE
    block_index = lax.broadcasted_iota(jnp.int32, (blocks, LANE), 0)
    lane_index = lax.broadcasted_iota(jnp.int32, (LANE, LANE), 0)
    for n, cells_ref in enumerate(cell_refs):
        place = cells_ref[...] - (at_ref[2] * rows - 2 * MAPX)
        block_of, lane_of = place >> 7, place & (LANE - 1)
        for o in range(each):
            block_hit = jnp.where(block_of[o : o + 1] == block_index, 1.0, 0.0).astype(jnp.bfloat16)
            lane_hit = jnp.where(lane_of[o : o + 1] == lane_index, 1.0, 0.0).astype(jnp.bfloat16)
            counts_ref[n * each + o] = lax.dot_general(
                block_hit, lane_hit, (((1,), (1,)), ((), ())), preferred_element_type=jnp.float32
            )

    def weights(k, m):
        return rows_ref[k : k + 1, MAPX * m : MAPX * (m + 1)]

    maps = [
        jnp.concatenate([counts_ref[:, 2 * m, :], counts_ref[:, 2 * m + 1, :]], axis=1)
        for m in range(window // MAPX)
    ]
    for first in (0, 1):
        moved = []
        for m in range(1, len(maps) - 1):
            t = m + first
            here = maps[m]
            value = weights(0, t) * here + pltpu.roll(weights(1, t) * here, MAPX - 1, 1)
            value = value + pltpu.roll(weights(2, t) * here, 1, 1)
            value = value + weights(3, t + 1) * maps[m + 1] + weights(4, t - 1) * maps[m - 1]
            moved.append(value)
        maps = moved
    for m, value in enumerate(maps):
        out_ref[:, MAPX * m : MAPX * (m + 1)] = value


def prepare(at, wind_mask, wind_speed, obs_cells, rows, cols, pieces, group=4):
    obs_count, foot = obs_cells.shape
    each = obs_count // pieces
    map_total = wind_speed.shape[1] // MAPX

    def kernel(*refs):
        prepare_kernel(rows, map_total, *refs)

    def fixed(shape):
        return pl.BlockSpec(shape, lambda s, a: (0, 0))

    col_shape = (8, cols + 2 * MAPX)
    down_shape = (rows + 2 * MAPX, 8)
    window = rows + 4 * MAPX
    return pl.pallas_call(
        kernel,
        out_shape=(
            jax.ShapeDtypeStruct((obs_count, rows), jnp.float32),
            jax.ShapeDtypeStruct(col_shape, jnp.float32),
            jax.ShapeDtypeStruct(down_shape, jnp.float32),
        ),
        grid_spec=pltpu.PrefetchScalarGridSpec(
            num_scalar_prefetch=1,
            grid=(pieces // group,),
            in_specs=[fixed(wind_mask.shape), fixed(wind_speed.shape)]
            + [
                pl.BlockSpec((each, foot), lambda s, a, n=n: (s * group + n ^ a[2], 0))
                for n in range(group)
            ],
            out_specs=(
                pl.BlockSpec((each * group, rows), lambda s, a: (s, 0)),
                fixed(col_shape),
                fixed(down_shape),
            ),
            scratch_shapes=[
                pltpu.VMEM((8, window), jnp.float32),
                pltpu.VMEM((each * group, window // LANE, LANE), jnp.float32),
            ],
        ),
        cost_estimate=pl.CostEstimate(flops=1 << 27, bytes_accessed=1 << 21, transcendentals=0),
        name="prepare",
    )(at, wind_mask, wind_speed, *[obs_cells] * group)


def step_cols(before, here, behind, weights):
    width = here.shape[1]
    result = weights[0] * here + weights[1] * pltpu.roll(here, 1, 1)
    result = result + weights[2] * pltpu.roll(here, width - 1, 1)
    return result + weights[3] * before + weights[4] * behind


def cols_kernel(inner, unroll, core_ref, here_ref, near_ref, *refs):
    far_refs, (weights_ref, out_ref) = refs[:-2], refs[-2:]
    first = core_ref[0] == 0

    def weights(m):
        return [weights_ref[k : k + 1, MAPX * m : MAPX * (m + 1)] for k in range(5)]

    def body(t, carry):
        rows = pl.ds(pl.multiple_of(t * inner, inner), inner)
        near, here = near_ref[rows, :], here_ref[rows, :]
        far = far_refs[0][rows, :]
        for ref in far_refs[1:]:
            far = far + ref[rows, :]
        west = jnp.where(first, far, near)
        east = jnp.where(first, near, far)
        maps = [part[:, MAPX * k : MAPX * (k + 1)] for part in (west, here, east) for k in range(2)]
        once = [step_cols(maps[m], maps[m + 1], maps[m + 2], weights(m)) for m in range(4)]
        for m in range(2):
            out_ref[rows, MAPX * m : MAPX * (m + 1)] = step_cols(
                once[m], once[m + 1], once[m + 2], weights(m + 1)
            )
        return carry

    lax.fori_loop(0, here_ref.shape[0] // inner, body, 0, unroll=unroll)


def move_cols(core, here, near, fars, weights, rows):
    cols = here[0].shape[1]
    tile = min(rows, 128)
    inner = min(rows, 64)
    steps = rows // tile

    def kernel(*refs):
        cols_kernel(inner, tile // inner, *refs)

    def spec(at):
        return pl.BlockSpec((tile, cols), lambda s, c: (at * steps + s, 0))

    blocks = [here, near, *fars]
    return pl.pallas_call(
        kernel,
        out_shape=jax.ShapeDtypeStruct((rows, cols), jnp.float32),
        grid_spec=pltpu.PrefetchScalarGridSpec(
            num_scalar_prefetch=1,
            grid=(steps,),
            in_specs=[spec(at) for _, at in blocks]
            + [pl.BlockSpec(weights.shape, lambda s, c: (0, 0))],
            out_specs=spec(0),
        ),
        compiler_params=SMALL,
        cost_estimate=pl.CostEstimate(
            flops=27 * rows * cols, bytes_accessed=16 * rows * cols, transcendentals=0
        ),
        name="move_cols",
    )(core, *[array for array, _ in blocks], weights)


def rows_kernel(chunk, *refs):
    maps, (update_ref, weights_ref, out_ref, once_ref) = refs[:7], refs[7:]

    def step(source, base, before, behind, weights_at, emit):
        def body(c, carry):
            start = pl.multiple_of(c * chunk, chunk)
            low = pl.multiple_of(jnp.maximum(start - 8, 0), 8)
            high = pl.multiple_of(jnp.minimum(start + chunk, MAPX - 8), 8)
            here = source[pl.ds(base + start, chunk), :]
            wide = jnp.concatenate(
                [source[pl.ds(base + low, 8), :], here, source[pl.ds(base + high, 8), :]], axis=0
            )
            weights = weights_ref[pl.ds(weights_at + start, chunk), :]
            value = weights[:, 0:1] * here
            value = value + weights[:, 1:2] * pltpu.roll(wide, 1, 0)[8 : 8 + chunk]
            value = value + weights[:, 2:3] * pltpu.roll(wide, chunk + 15, 0)[8 : 8 + chunk]
            if before is not None:
                value = value + weights[:, 3:4] * before[0][pl.ds(before[1] + start, chunk), :]
            value = value + weights[:, 4:5] * behind[0][pl.ds(behind[1] + start, chunk), :]
            emit(start, value)
            return carry

        lax.fori_loop(0, MAPX // chunk, body, 0, unroll=MAPX // chunk)

    for m in range(6):

        def emit(start, value, m=m):
            once_ref[pl.ds(MAPX * m + start, chunk), :] = value

        step(maps[m], 0, (maps[m - 1], 0) if m > 0 else None, (maps[m + 1], 0), MAPX * m, emit)
    for m in range(1, 5):

        def emit(start, value, m=m):
            rows = pl.ds(MAPX * (m - 1) + start, chunk)
            out_ref[rows, :] = value - update_ref[rows, :]

        step(
            once_ref, MAPX * m, (once_ref, MAPX * (m - 1)), (once_ref, MAPX * (m + 1)), MAPX * m, emit
        )


def move_rows(maps, update, weights):
    rows, cols = update.shape

    def kernel(above, first, third, fourth, below, *refs):
        halves = [ref.at[pl.ds(MAPX * k, MAPX), :] for ref in (first, below) for k in range(2)]
        rows_kernel(64, above, *halves[:2], third, fourth, *halves[2:], *refs)

    def whole(array):
        return pl.BlockSpec(array.shape, lambda s: (0, 0))

    return pl.pallas_call(
        kernel,
        out_shape=jax.ShapeDtypeStruct((rows, cols), jnp.float32),
        grid=(1,),
        in_specs=[whole(array) for array in (*maps, update, weights)],
        out_specs=whole(update),
        scratch_shapes=[pltpu.VMEM((rows + 2 * MAPX, cols), jnp.float32)],
        compiler_params=SMALL,
        cost_estimate=pl.CostEstimate(
            flops=24 * rows * cols, bytes_accessed=16 * rows * cols, transcendentals=0
        ),
        name="move_rows",
    )(*maps, update, weights)


def last_kernel(result_ref, halo_ref, weights_ref, before_ref, out_ref):
    factor = weights_ref[:, 3:4] * before_ref[:, 3:4]
    out_ref[...] = result_ref[...] + factor * halo_ref[...]


def add_last(result, halo, weights):
    cols = result.shape[1]
    tile = 128
    steps = MAPX // tile
    block = pl.BlockSpec((tile, cols), lambda s: (s, 0))
    return pl.pallas_call(
        last_kernel,
        out_shape=jax.ShapeDtypeStruct(result.shape, result.dtype),
        grid=(steps,),
        in_specs=[
            block,
            block,
            pl.BlockSpec((tile, weights.shape[1]), lambda s: (steps + s, 0)),
            pl.BlockSpec((tile, weights.shape[1]), lambda s: (s, 0)),
        ],
        out_specs=block,
        input_output_aliases={0: 0},
        compiler_params=SMALL,
        cost_estimate=pl.CostEstimate(
            flops=2 * MAPX * cols, bytes_accessed=12 * MAPX * cols, transcendentals=0
        ),
        name="add_last",
    )(result, halo, weights, weights)


def local(covariance, wind_mask, wind_speed, obs_cells, obs_scale, gain):
    rows, cols = covariance.shape
    row_parts = lax.axis_size("row")
    col_parts = lax.axis_size("col")
    assert row_parts == 16 and rows == 4 * MAPX and cols == 2 * MAPX
    row_at = lax.axis_index("row")
    col_at = lax.axis_index("col")
    down = [(i, i + 1) for i in range(row_parts - 1)]
    up = [(i + 1, i) for i in range(row_parts - 1)]
    near_swap = [(j, j ^ 1) for j in range(col_parts)]
    far_swap = [(j, (j - 1 ^ 1) + 1) for j in range(1, col_parts - 1)]
    turning = [(a, b) for a, b in far_swap if a % 4 in (0, 3)]
    straight = [(a, b) for a, b in far_swap if a % 4 in (1, 2)]
    core = (col_at % 2).reshape(1)
    at = jnp.stack([row_at * (rows // MAPX), col_at * (cols // MAPX), row_at])

    def across(bit):
        return [(i, i ^ bit) for i in range(row_parts)]

    far_turning = lax.ppermute(covariance, "col", turning)
    near = lax.ppermute(covariance, "col", near_swap)

    select, col_weights, down_weights = prepare(
        at, wind_mask, wind_speed, obs_cells, rows, cols, row_parts
    )
    part = jnp.dot(select, covariance, precision=HIGH, preferred_element_type=jnp.float32)

    def sum_over(value, bits):
        size = value.shape[0] // (len(bits) + 1)
        total = value[:size]
        for n, bit in enumerate(bits, 1):
            piece = value[size * n : size * (n + 1)]
            total = total + lax.ppermute(piece, "row", across(bit))
        return total

    def all_of(value, bits):
        return [value] + [lax.ppermute(value, "row", across(bit)) for bit in bits]

    total = sum_over(part, X_BITS)
    total = sum_over(total, Z_BITS)
    each = total.shape[0]

    late = after(covariance, select)

    def far_part(start, size):
        return lax.ppermute(along(late, start, size, 0), "col", straight)

    piece_far = lax.ppermute(total, "col", far_swap)
    far_straight = {"far_up": far_part(0, 2 * MAPX)}
    piece_near = lax.ppermute(total, "col", near_swap)
    piece = move_cols(core, (total, 0), (piece_near, 0), [(piece_far, 0)], col_weights, each)
    observed = all_of(piece, Z_BITS)
    far_straight["far3"] = far_part(3 * MAPX, MAPX)
    far_straight["far2"] = far_part(2 * MAPX, MAPX)

    def move(name, block, size, *earlier):
        return move_cols(
            core,
            (covariance, block),
            (near, block),
            [(far_turning, block), (after(far_straight[name], *earlier), 0)],
            col_weights,
            size,
        )

    moved_up = move("far_up", 0, 2 * MAPX)
    halo_up = lax.ppermute(moved_up, "row", up)
    observed = jnp.concatenate([after(observed[0], moved_up), *observed[1:]])
    observed = jnp.concatenate(all_of(observed, X_BITS))
    index = jnp.arange(gain.shape[1], dtype=jnp.int32)
    reorder = (index[:, None] ^ (row_at * each)) == index[None, :]
    ordered_gain = jnp.dot(gain, reorder.astype(gain.dtype), preferred_element_type=jnp.float32)
    ordered_scale = jnp.sum(jnp.where(reorder, obs_scale[:, None], 0.0), axis=0)
    ordered_gain = ordered_gain * ordered_scale[None, :]

    moved3 = move("far3", 3, MAPX)
    halo3 = lax.ppermute(moved3, "row", down)
    update = jnp.dot(
        ordered_gain,
        after(observed, moved3),
        precision=HIGH,
        preferred_element_type=jnp.float32,
    )
    moved2 = move("far2", 2, MAPX, update)
    halo2 = lax.ppermute(moved2, "row", down)

    result = move_rows([halo3, moved_up, moved2, moved3, halo_up], update, down_weights)
    return add_last(result, halo2, down_weights)


X_BITS = (4, 8, 12)
Z_BITS = (1, 2, 3)


def solution(mesh):
    placed = (P("row", "col"), P(), P(), P(), P(), P("row", None))
    return jax.shard_map(
        local, mesh=mesh, in_specs=placed, out_specs=P("row", "col"), check_vma=False
    )
```

```python
import jax
import jax.numpy as jnp
from jax import lax
from jax.experimental import pallas as pl
from jax.experimental.pallas import tpu as pltpu
from jax.sharding import PartitionSpec as P


MAPX = 256
LANE = 128


diffusion = 0.05
HIGH = lax.Precision.HIGHEST
SMALL = pltpu.CompilerParams(vmem_limit_bytes=16 << 20)


def after(value, *earlier):
    return lax.optimization_barrier((value,) + earlier)[0]


def weights_table(map_total, map_row, mask_ref, speed_ref):
    inside = (map_row >= 0) & (map_row < map_total)
    cells = pl.ds(pl.multiple_of(jnp.clip(map_row, 0, map_total - 1) * MAPX, MAPX), MAPX)
    speed = speed_ref[:, cells]
    sign = mask_ref[:, cells].astype(jnp.float32)
    column = lax.broadcasted_iota(jnp.int32, (1, MAPX), 1)
    speed_x, speed_y = speed[0:1], speed[1:2]
    sign_x, sign_y = sign[0:1], sign[1:2]
    middle = 1.0 - speed_x - speed_y - 4.0 * diffusion
    western = jnp.where(column > 0, speed_x * sign_x + diffusion, 0.0)
    eastern = jnp.where(column < MAPX - 1, speed_x * (1.0 - sign_x) + diffusion, 0.0)
    northern = jnp.where(map_row > 0, speed_y * sign_y + diffusion, 0.0)
    southern = jnp.where(map_row < map_total - 1, speed_y * (1.0 - sign_y) + diffusion, 0.0)
    zero = jnp.zeros_like(middle)
    table = jnp.concatenate(
        [middle, western, eastern, northern, southern, zero, zero, zero], axis=0
    )
    return jnp.where(inside, table, 0.0)


def prepare_kernel(rows, map_total, at_ref, mask_ref, speed_ref, *refs):
    cell_refs, (out_ref, cols_ref, down_ref, rows_ref, counts_ref) = refs[:-5], refs[-5:]

    @pl.when(pl.program_id(0) == 0)
    def _():
        last = rows_ref.shape[1] // MAPX - 1
        for m in range(last + 1):
            table = weights_table(map_total, at_ref[0] + m - 2, mask_ref, speed_ref)
            rows_ref[:, MAPX * m : MAPX * (m + 1)] = table
            if 0 < m < last:
                down_ref[MAPX * (m - 1) : MAPX * m, :] = table.T
        for m in range(cols_ref.shape[1] // MAPX):
            cols_ref[:, MAPX * m : MAPX * (m + 1)] = weights_table(
                map_total, at_ref[1] + m - 1, mask_ref, speed_ref
            )

    each = cell_refs[0].shape[0]
    window = rows_ref.shape[1]
    blocks = window // LANE
    block_index = lax.broadcasted_iota(jnp.int32, (blocks, LANE), 0)
    lane_index = lax.broadcasted_iota(jnp.int32, (LANE, LANE), 0)
    for n, cells_ref in enumerate(cell_refs):
        place = cells_ref[...] - (at_ref[2] * rows - 2 * MAPX)
        block_of, lane_of = place >> 7, place & (LANE - 1)
        for o in range(each):
            block_hit = jnp.where(block_of[o : o + 1] == block_index, 1.0, 0.0).astype(jnp.bfloat16)
            lane_hit = jnp.where(lane_of[o : o + 1] == lane_index, 1.0, 0.0).astype(jnp.bfloat16)
            counts_ref[n * each + o] = lax.dot_general(
                block_hit, lane_hit, (((1,), (1,)), ((), ())), preferred_element_type=jnp.float32
            )

    def weights(k, m):
        return rows_ref[k : k + 1, MAPX * m : MAPX * (m + 1)]

    maps = [
        jnp.concatenate([counts_ref[:, 2 * m, :], counts_ref[:, 2 * m + 1, :]], axis=1)
        for m in range(window // MAPX)
    ]
    for first in (0, 1):
        moved = []
        for m in range(1, len(maps) - 1):
            t = m + first
            here = maps[m]
            value = weights(0, t) * here + pltpu.roll(weights(1, t) * here, MAPX - 1, 1)
            value = value + pltpu.roll(weights(2, t) * here, 1, 1)
            value = value + weights(3, t + 1) * maps[m + 1] + weights(4, t - 1) * maps[m - 1]
            moved.append(value)
        maps = moved
    for m, value in enumerate(maps):
        out_ref[:, MAPX * m : MAPX * (m + 1)] = value


def prepare(at, wind_mask, wind_speed, obs_cells, rows, cols, pieces, group=4):
    obs_count, foot = obs_cells.shape
    each = obs_count // pieces
    map_total = wind_speed.shape[1] // MAPX

    def kernel(*refs):
        prepare_kernel(rows, map_total, *refs)

    def fixed(shape):
        return pl.BlockSpec(shape, lambda s, a: (0, 0))

    col_shape = (8, cols + 2 * MAPX)
    down_shape = (rows + 2 * MAPX, 8)
    window = rows + 4 * MAPX
    return pl.pallas_call(
        kernel,
        out_shape=(
            jax.ShapeDtypeStruct((obs_count, rows), jnp.float32),
            jax.ShapeDtypeStruct(col_shape, jnp.float32),
            jax.ShapeDtypeStruct(down_shape, jnp.float32),
        ),
        grid_spec=pltpu.PrefetchScalarGridSpec(
            num_scalar_prefetch=1,
            grid=(pieces // group,),
            in_specs=[fixed(wind_mask.shape), fixed(wind_speed.shape)]
            + [
                pl.BlockSpec((each, foot), lambda s, a, n=n: (s * group + n ^ a[2], 0))
                for n in range(group)
            ],
            out_specs=(
                pl.BlockSpec((each * group, rows), lambda s, a: (s, 0)),
                fixed(col_shape),
                fixed(down_shape),
            ),
            scratch_shapes=[
                pltpu.VMEM((8, window), jnp.float32),
                pltpu.VMEM((each * group, window // LANE, LANE), jnp.float32),
            ],
        ),
        cost_estimate=pl.CostEstimate(flops=1 << 27, bytes_accessed=1 << 21, transcendentals=0),
        name="prepare",
    )(at, wind_mask, wind_speed, *[obs_cells] * group)


def step_cols(before, here, behind, weights):
    width = here.shape[1]
    result = weights[0] * here + weights[1] * pltpu.roll(here, 1, 1)
    result = result + weights[2] * pltpu.roll(here, width - 1, 1)
    return result + weights[3] * before + weights[4] * behind


def cols_kernel(inner, unroll, at_ref, here_ref, near_ref, *refs):
    far_refs, (weights_ref, out_ref) = refs[:-2], refs[-2:]
    first = at_ref[0] == 0

    def weights(m):
        return [weights_ref[k : k + 1, MAPX * m : MAPX * (m + 1)] for k in range(5)]

    def body(t, carry):
        rows = pl.ds(pl.multiple_of(t * inner, inner), inner)
        near, here = near_ref[rows, :], here_ref[rows, :]
        far = far_refs[0][rows, :]
        for ref in far_refs[1:]:
            far = far + ref[rows, :]
        west = jnp.where(first, far, near)
        east = jnp.where(first, near, far)
        maps = [part[:, MAPX * k : MAPX * (k + 1)] for part in (west, here, east) for k in range(2)]
        once = [step_cols(maps[m], maps[m + 1], maps[m + 2], weights(m)) for m in range(4)]
        for m in range(2):
            out_ref[rows, MAPX * m : MAPX * (m + 1)] = step_cols(
                once[m], once[m + 1], once[m + 2], weights(m + 1)
            )
        return carry

    lax.fori_loop(0, here_ref.shape[0] // inner, body, 0, unroll=unroll)


def move_cols(at, here, near, fars, weights, rows):
    cols = here[0].shape[1]
    tile = min(rows, 128)
    inner = min(rows, 64)
    steps = rows // tile

    def kernel(*refs):
        cols_kernel(inner, tile // inner, *refs)

    def spec(block):
        if isinstance(block, str):
            entry = HALVES[block]
            return pl.BlockSpec((tile, cols), lambda s, a: (a[entry] * steps + s, 0))
        return pl.BlockSpec((tile, cols), lambda s, a: (block * steps + s, 0))

    blocks = [here, near, *fars]
    return pl.pallas_call(
        kernel,
        out_shape=jax.ShapeDtypeStruct((rows, cols), jnp.float32),
        grid_spec=pltpu.PrefetchScalarGridSpec(
            num_scalar_prefetch=1,
            grid=(steps,),
            in_specs=[spec(block) for _, block in blocks]
            + [pl.BlockSpec(weights.shape, lambda s, a: (0, 0))],
            out_specs=spec(0),
        ),
        compiler_params=SMALL,
        cost_estimate=pl.CostEstimate(
            flops=27 * rows * cols, bytes_accessed=16 * rows * cols, transcendentals=0
        ),
        name="move_cols",
    )(at, *[array for array, _ in blocks], weights)


def load(parts, start, size):
    value = None
    for ref, base in parts:
        part = ref[pl.ds(base + start, size), :]
        value = part if value is None else value + part
    return value


def step_rows(chunk, before, here, behind, weights_ref, weights_at, emit):
    def body(c, carry):
        start = pl.multiple_of(c * chunk, chunk)
        low = pl.multiple_of(jnp.maximum(start - 8, 0), 8)
        high = pl.multiple_of(jnp.minimum(start + chunk, MAPX - 8), 8)
        weights = weights_ref[pl.ds(weights_at + start, chunk), :]
        terms = []
        if here:
            center = load(here, start, chunk)
            wide = jnp.concatenate([load(here, low, 8), center, load(here, high, 8)], axis=0)
            terms.append(weights[:, 0:1] * center)
            terms.append(weights[:, 1:2] * pltpu.roll(wide, 1, 0)[8 : 8 + chunk])
            terms.append(weights[:, 2:3] * pltpu.roll(wide, chunk + 15, 0)[8 : 8 + chunk])
        if before:
            terms.append(weights[:, 3:4] * load(before, start, chunk))
        if behind:
            terms.append(weights[:, 4:5] * load(behind, start, chunk))
        value = terms[0]
        for term in terms[1:]:
            value = value + term
        emit(start, value)
        return carry

    lax.fori_loop(0, MAPX // chunk, body, 0, unroll=MAPX // chunk)


def two(*refs):
    return [[(ref, MAPX * k) for ref in refs] for k in range(2)]


def rows_kernel(chunk, at_ref, a_ref, b_ref, one_ref, other_ref, update_ref, weights_ref, out_ref, once_ref):
    def run(maps):
        once = {}
        for m in range(1, 7):
            at = MAPX * (m - 1)

            def emit(start, value, at=at):
                once_ref[pl.ds(at + start, chunk), :] = value

            step_rows(chunk, maps[m - 1], maps[m], maps[m + 1], weights_ref, at, emit)
            once[m] = [(once_ref, at)]
        for m in range(2, 6):
            at = MAPX * (m - 2)

            def emit(start, value, at=at):
                rows = pl.ds(at + start, chunk)
                out_ref[rows, :] = value - update_ref[rows, :]

            step_rows(chunk, once[m - 1], once[m], once[m + 1], weights_ref, MAPX * (m - 1), emit)

    odd = at_ref[HALVES["first"]] == 1
    none = [[], []]

    @pl.when(odd)
    def _():
        run(none + two(b_ref) + two(a_ref) + two(one_ref, other_ref))

    @pl.when(jnp.logical_not(odd))
    def _():
        run(two(one_ref, other_ref) + two(a_ref) + two(b_ref) + none)


def move_rows(at, first, second, halo, update, weights):
    rows, cols = update.shape

    def kernel(*refs):
        rows_kernel(64, *refs)

    def whole(array):
        return pl.BlockSpec(array.shape, lambda s, a: (0, 0))

    return pl.pallas_call(
        kernel,
        out_shape=jax.ShapeDtypeStruct((rows, cols), jnp.float32),
        grid_spec=pltpu.PrefetchScalarGridSpec(
            num_scalar_prefetch=1,
            grid=(1,),
            in_specs=[whole(array) for array in (first, second, *halo, update, weights)],
            out_specs=whole(update),
            scratch_shapes=[pltpu.VMEM((rows + 2 * MAPX, cols), jnp.float32)],
        ),
        compiler_params=pltpu.CompilerParams(vmem_limit_bytes=20 << 20),
        cost_estimate=pl.CostEstimate(
            flops=24 * rows * cols, bytes_accessed=16 * rows * cols, transcendentals=0
        ),
        name="move_rows",
    )(at, first, second, *halo, update, weights)


def last_kernel(chunk, at_ref, result_ref, one_ref, other_ref, weights_ref, out_ref, once_ref):
    near, far = [(once_ref, 0)], [(once_ref, MAPX)]

    def into(at):
        def emit(start, value):
            once_ref[pl.ds(at + start, chunk), :] = value

        return emit

    def add(at):
        def emit(start, value):
            rows = pl.ds(at + start, chunk)
            out_ref[rows, :] = result_ref[rows, :] + value

        return emit

    def step(before, here, behind, m, emit):
        step_rows(chunk, before, here, behind, weights_ref, MAPX * (m - 1), emit)

    odd = at_ref[HALVES["first"]] == 1
    halo = two(one_ref, other_ref)

    @pl.when(odd)
    def _():
        step(halo[0], halo[1], [], 1, into(MAPX))
        step(halo[1], [], [], 2, into(0))
        step(far, near, [], 2, add(0))
        step(near, [], [], 3, add(MAPX))

    @pl.when(jnp.logical_not(odd))
    def _():
        step([], halo[0], halo[1], 6, into(MAPX))
        step([], [], halo[0], 5, into(0))
        step([], near, far, 5, add(MAPX))
        step([], [], near, 4, add(0))


def add_last(at, result, halo, weights):
    rows, cols = result.shape
    tile = 256
    block = pl.BlockSpec((rows // 2, tile), lambda s, a: (a[HALVES["second"]], s))
    part = pl.BlockSpec((rows // 2, tile), lambda s, a: (0, s))

    def kernel(*refs):
        last_kernel(64, *refs)

    return pl.pallas_call(
        kernel,
        out_shape=jax.ShapeDtypeStruct(result.shape, result.dtype),
        grid_spec=pltpu.PrefetchScalarGridSpec(
            num_scalar_prefetch=1,
            grid=(cols // tile,),
            in_specs=[block, part, part, pl.BlockSpec(weights.shape, lambda s, a: (0, 0))],
            out_specs=block,
            scratch_shapes=[pltpu.VMEM((2 * MAPX, tile), jnp.float32)],
        ),
        input_output_aliases={1: 0},
        compiler_params=SMALL,
        cost_estimate=pl.CostEstimate(
            flops=10 * rows * cols, bytes_accessed=8 * rows * cols, transcendentals=0
        ),
        name="add_last",
    )(at, result, *halo, weights)


def local(covariance, wind_mask, wind_speed, obs_cells, obs_scale, gain):
    rows, cols = covariance.shape
    row_parts = lax.axis_size("row")
    col_parts = lax.axis_size("col")
    assert row_parts == 16 and rows == 4 * MAPX and cols == 2 * MAPX
    row_at = lax.axis_index("row")
    col_at = lax.axis_index("col")
    near_swap = [(j, j ^ 1) for j in range(col_parts)]
    far_swap = [(j, (j - 1 ^ 1) + 1) for j in range(1, col_parts - 1)]
    turning = [(a, b) for a, b in far_swap if a % 4 in (0, 3)]
    straight = [(a, b) for a, b in far_swap if a % 4 in (1, 2)]
    first, second = row_at % 2, 1 - row_at % 2
    at = jnp.stack([row_at * (rows // MAPX), col_at * (cols // MAPX), row_at])
    place = jnp.stack([col_at % 2, first, second])
    half = rows // 2

    def row_swap(odd, kinds):
        cells = [(i, (i - odd ^ 1) + odd) for i in range(odd, row_parts - odd)]
        columns = [j for j in range(col_parts) if j % 4 in kinds]
        return [(a * col_parts + j, b * col_parts + j) for a, b in cells for j in columns]

    def across(bit):
        return [(i, i ^ bit) for i in range(row_parts)]

    far_turning = lax.ppermute(covariance, "col", turning)
    near = lax.ppermute(covariance, "col", near_swap)

    def far_part(number, source):
        block = lax.dynamic_slice_in_dim(source, number * half, half, 0)
        return lax.ppermute(block, "col", straight)

    far_first = far_part(first, covariance)

    select, col_weights, down_weights = prepare(
        at, wind_mask, wind_speed, obs_cells, rows, cols, row_parts
    )
    part = jnp.dot(select, covariance, precision=HIGH, preferred_element_type=jnp.float32)

    def sum_over(value, bits):
        size = value.shape[0] // (len(bits) + 1)
        total = value[:size]
        for n, bit in enumerate(bits, 1):
            piece = value[size * n : size * (n + 1)]
            total = total + lax.ppermute(piece, "row", across(bit))
        return total

    def all_of(value, bits):
        return [value] + [lax.ppermute(value, "row", across(bit)) for bit in bits]

    total = sum_over(part, X_BITS)
    total = sum_over(total, Z_BITS)
    each = total.shape[0]

    def move(block, *straight_parts):
        fars = [(far_turning, block)] + [(part, 0) for part in straight_parts]
        return move_cols(place, (covariance, block), (near, block), fars, col_weights, half)

    def swap_rows(block, odd, kinds):
        return lax.ppermute(block, ("row", "col"), row_swap(odd, kinds))

    early_first = move("first")
    early_second = move("second")
    piece_far = lax.ppermute(total, "col", far_swap)
    far_second = far_part(second, after(covariance, early_second))
    halo_first = [swap_rows(early_first, 1, (0, 3))]
    halo_second = [swap_rows(early_second, 0, (0, 3))]

    moved_first = move("first", far_first)
    halo_first.append(swap_rows(moved_first, 1, (1, 2)))
    piece_near = lax.ppermute(total, "col", near_swap)
    piece = move_cols(place, (total, 0), (piece_near, 0), [(piece_far, 0)], col_weights, each)
    observed = all_of(piece, Z_BITS)
    moved_second = move("second", far_second)
    halo_second.append(swap_rows(moved_second, 0, (1, 2)))

    observed = jnp.concatenate([after(observed[0], moved_second), *observed[1:]])
    observed = jnp.concatenate(all_of(observed, X_BITS))
    index = jnp.arange(gain.shape[1], dtype=jnp.int32)
    reorder = (index[:, None] ^ (row_at * each)) == index[None, :]
    ordered_gain = jnp.dot(gain, reorder.astype(gain.dtype), preferred_element_type=jnp.float32)
    ordered_scale = jnp.sum(jnp.where(reorder, obs_scale[:, None], 0.0), axis=0)
    ordered_gain = ordered_gain * ordered_scale[None, :]
    update = jnp.dot(ordered_gain, observed, precision=HIGH, preferred_element_type=jnp.float32)

    result = move_rows(place, moved_first, moved_second, halo_first, update, down_weights)
    return add_last(place, result, halo_second, down_weights)


HALVES = {"first": 1, "second": 2}
X_BITS = (4, 8, 12)
Z_BITS = (1, 2, 3)


def solution(mesh):
    placed = (P("row", "col"), P(), P(), P(), P(), P("row", None))
    return jax.shard_map(
        local, mesh=mesh, in_specs=placed, out_specs=P("row", "col"), check_vma=False
    )
```

```python
import jax
import jax.numpy as jnp
from jax import lax
from jax.experimental import pallas as pl
from jax.experimental.pallas import tpu as pltpu
from jax.sharding import PartitionSpec as P


MAPX = 256
LANE = 128


diffusion = 0.05
HIGH = lax.Precision.HIGHEST
SMALL = pltpu.CompilerParams(vmem_limit_bytes=16 << 20)


def after(value, *earlier):
    return lax.optimization_barrier((value,) + earlier)[0]


def weights_table(map_total, map_row, mask_ref, speed_ref):
    inside = (map_row >= 0) & (map_row < map_total)
    cells = pl.ds(pl.multiple_of(jnp.clip(map_row, 0, map_total - 1) * MAPX, MAPX), MAPX)
    speed = speed_ref[:, cells]
    sign = mask_ref[:, cells].astype(jnp.float32)
    column = lax.broadcasted_iota(jnp.int32, (1, MAPX), 1)
    speed_x, speed_y = speed[0:1], speed[1:2]
    sign_x, sign_y = sign[0:1], sign[1:2]
    middle = 1.0 - speed_x - speed_y - 4.0 * diffusion
    western = jnp.where(column > 0, speed_x * sign_x + diffusion, 0.0)
    eastern = jnp.where(column < MAPX - 1, speed_x * (1.0 - sign_x) + diffusion, 0.0)
    northern = jnp.where(map_row > 0, speed_y * sign_y + diffusion, 0.0)
    southern = jnp.where(map_row < map_total - 1, speed_y * (1.0 - sign_y) + diffusion, 0.0)
    zero = jnp.zeros_like(middle)
    table = jnp.concatenate(
        [middle, western, eastern, northern, southern, zero, zero, zero], axis=0
    )
    return jnp.where(inside, table, 0.0)


def prepare_kernel(rows, map_total, at_ref, mask_ref, speed_ref, *refs):
    cell_refs, (out_ref, cols_ref, down_ref, rows_ref, counts_ref) = refs[:-5], refs[-5:]

    @pl.when(pl.program_id(0) == 0)
    def _():
        last = rows_ref.shape[1] // MAPX - 1
        for m in range(last + 1):
            table = weights_table(map_total, at_ref[0] + m - 2, mask_ref, speed_ref)
            rows_ref[:, MAPX * m : MAPX * (m + 1)] = table
            if 0 < m < last:
                down_ref[MAPX * (m - 1) : MAPX * m, :] = table.T
        for m in range(cols_ref.shape[1] // MAPX):
            cols_ref[:, MAPX * m : MAPX * (m + 1)] = weights_table(
                map_total, at_ref[1] + m - 1, mask_ref, speed_ref
            )

    each = cell_refs[0].shape[0]
    window = rows_ref.shape[1]
    blocks = window // LANE
    block_index = lax.broadcasted_iota(jnp.int32, (blocks, LANE), 0)
    lane_index = lax.broadcasted_iota(jnp.int32, (LANE, LANE), 0)
    for n, cells_ref in enumerate(cell_refs):
        place = cells_ref[...] - (at_ref[2] * rows - 2 * MAPX)
        block_of, lane_of = place >> 7, place & (LANE - 1)
        for o in range(each):
            block_hit = jnp.where(block_of[o : o + 1] == block_index, 1.0, 0.0).astype(jnp.bfloat16)
            lane_hit = jnp.where(lane_of[o : o + 1] == lane_index, 1.0, 0.0).astype(jnp.bfloat16)
            counts_ref[n * each + o] = lax.dot_general(
                block_hit, lane_hit, (((1,), (1,)), ((), ())), preferred_element_type=jnp.float32
            )

    def weights(k, m):
        return rows_ref[k : k + 1, MAPX * m : MAPX * (m + 1)]

    maps = [
        jnp.concatenate([counts_ref[:, 2 * m, :], counts_ref[:, 2 * m + 1, :]], axis=1)
        for m in range(window // MAPX)
    ]
    for first in (0, 1):
        moved = []
        for m in range(1, len(maps) - 1):
            t = m + first
            here = maps[m]
            value = weights(0, t) * here + pltpu.roll(weights(1, t) * here, MAPX - 1, 1)
            value = value + pltpu.roll(weights(2, t) * here, 1, 1)
            value = value + weights(3, t + 1) * maps[m + 1] + weights(4, t - 1) * maps[m - 1]
            moved.append(value)
        maps = moved
    for m, value in enumerate(maps):
        out_ref[:, MAPX * m : MAPX * (m + 1)] = value


def prepare(at, wind_mask, wind_speed, obs_cells, rows, cols, pieces, group=4):
    obs_count, foot = obs_cells.shape
    each = obs_count // pieces
    map_total = wind_speed.shape[1] // MAPX

    def kernel(*refs):
        prepare_kernel(rows, map_total, *refs)

    def fixed(shape):
        return pl.BlockSpec(shape, lambda s, a: (0, 0))

    col_shape = (8, cols + 2 * MAPX)
    down_shape = (rows + 2 * MAPX, 8)
    window = rows + 4 * MAPX
    return pl.pallas_call(
        kernel,
        out_shape=(
            jax.ShapeDtypeStruct((obs_count, rows), jnp.float32),
            jax.ShapeDtypeStruct(col_shape, jnp.float32),
            jax.ShapeDtypeStruct(down_shape, jnp.float32),
        ),
        grid_spec=pltpu.PrefetchScalarGridSpec(
            num_scalar_prefetch=1,
            grid=(pieces // group,),
            in_specs=[fixed(wind_mask.shape), fixed(wind_speed.shape)]
            + [
                pl.BlockSpec((each, foot), lambda s, a, n=n: (s * group + n ^ a[2], 0))
                for n in range(group)
            ],
            out_specs=(
                pl.BlockSpec((each * group, rows), lambda s, a: (s, 0)),
                fixed(col_shape),
                fixed(down_shape),
            ),
            scratch_shapes=[
                pltpu.VMEM((8, window), jnp.float32),
                pltpu.VMEM((each * group, window // LANE, LANE), jnp.float32),
            ],
        ),
        cost_estimate=pl.CostEstimate(flops=1 << 27, bytes_accessed=1 << 21, transcendentals=0),
        name="prepare",
    )(at, wind_mask, wind_speed, *[obs_cells] * group)


def step_cols(before, here, behind, weights):
    width = here.shape[1]
    result = weights[0] * here + weights[1] * pltpu.roll(here, 1, 1)
    result = result + weights[2] * pltpu.roll(here, width - 1, 1)
    return result + weights[3] * before + weights[4] * behind


def cols_kernel(inner, unroll, at_ref, here_ref, near_ref, *refs):
    far_refs, (weights_ref, out_ref) = refs[:-2], refs[-2:]
    first = at_ref[0] == 0

    def weights(m):
        return [weights_ref[k : k + 1, MAPX * m : MAPX * (m + 1)] for k in range(5)]

    def body(t, carry):
        rows = pl.ds(pl.multiple_of(t * inner, inner), inner)
        near, here = near_ref[rows, :], here_ref[rows, :]
        far = far_refs[0][rows, :]
        for ref in far_refs[1:]:
            far = far + ref[rows, :]
        west = jnp.where(first, far, near)
        east = jnp.where(first, near, far)
        maps = [part[:, MAPX * k : MAPX * (k + 1)] for part in (west, here, east) for k in range(2)]
        once = [step_cols(maps[m], maps[m + 1], maps[m + 2], weights(m)) for m in range(4)]
        for m in range(2):
            out_ref[rows, MAPX * m : MAPX * (m + 1)] = step_cols(
                once[m], once[m + 1], once[m + 2], weights(m + 1)
            )
        return carry

    lax.fori_loop(0, here_ref.shape[0] // inner, body, 0, unroll=unroll)


def move_cols(at, here, near, fars, weights, rows, only=None):
    cols = here[0].shape[1]
    tile = min(rows, 128)
    inner = min(rows, 64)
    steps = rows // tile

    def kernel(at_ref, *refs):
        if only is None:
            cols_kernel(inner, tile // inner, at_ref, *refs)
        else:

            @pl.when(at_ref[HALVES[only]] == 1)
            def _():
                cols_kernel(inner, tile // inner, at_ref, *refs)

    def spec(block):
        def index(s, a):
            at_block = a[HALVES[block]] if isinstance(block, str) else block
            row = at_block * steps + s
            return (row if only is None else row * a[HALVES[only]], 0)

        return pl.BlockSpec((tile, cols), index)

    blocks = [here, near, *fars]
    return pl.pallas_call(
        kernel,
        out_shape=jax.ShapeDtypeStruct((rows, cols), jnp.float32),
        grid_spec=pltpu.PrefetchScalarGridSpec(
            num_scalar_prefetch=1,
            grid=(steps,),
            in_specs=[spec(block) for _, block in blocks]
            + [pl.BlockSpec(weights.shape, lambda s, a: (0, 0))],
            out_specs=spec(0),
        ),
        compiler_params=SMALL,
        cost_estimate=pl.CostEstimate(
            flops=27 * rows * cols, bytes_accessed=16 * rows * cols, transcendentals=0
        ),
        name="move_cols",
    )(at, *[array for array, _ in blocks], weights)


def load(parts, start, size):
    value = None
    for ref, base in parts:
        part = ref[pl.ds(base + start, size), :]
        value = part if value is None else value + part
    return value


def step_rows(chunk, before, here, behind, weights_ref, weights_at, emit):
    def body(c, carry):
        start = pl.multiple_of(c * chunk, chunk)
        low = pl.multiple_of(jnp.maximum(start - 8, 0), 8)
        high = pl.multiple_of(jnp.minimum(start + chunk, MAPX - 8), 8)
        weights = weights_ref[pl.ds(weights_at + start, chunk), :]
        terms = []
        if here:
            center = load(here, start, chunk)
            wide = jnp.concatenate([load(here, low, 8), center, load(here, high, 8)], axis=0)
            terms.append(weights[:, 0:1] * center)
            terms.append(weights[:, 1:2] * pltpu.roll(wide, 1, 0)[8 : 8 + chunk])
            terms.append(weights[:, 2:3] * pltpu.roll(wide, chunk + 15, 0)[8 : 8 + chunk])
        if before:
            terms.append(weights[:, 3:4] * load(before, start, chunk))
        if behind:
            terms.append(weights[:, 4:5] * load(behind, start, chunk))
        value = terms[0]
        for term in terms[1:]:
            value = value + term
        emit(start, value)
        return carry

    lax.fori_loop(0, MAPX // chunk, body, 0, unroll=MAPX // chunk)


def two(*refs):
    return [[(ref, MAPX * k) for ref in refs] for k in range(2)]


def rows_kernel(chunk, at_ref, a_ref, b_ref, one_ref, other_ref, update_ref, weights_ref, out_ref, once_ref):
    def run(maps):
        once = {}
        for m in range(1, 7):
            at = MAPX * (m - 1)

            def emit(start, value, at=at):
                once_ref[pl.ds(at + start, chunk), :] = value

            step_rows(chunk, maps[m - 1], maps[m], maps[m + 1], weights_ref, at, emit)
            once[m] = [(once_ref, at)]
        for m in range(2, 6):
            at = MAPX * (m - 2)

            def emit(start, value, at=at):
                rows = pl.ds(at + start, chunk)
                out_ref[rows, :] = value - update_ref[rows, :]

            step_rows(chunk, once[m - 1], once[m], once[m + 1], weights_ref, MAPX * (m - 1), emit)

    odd = at_ref[HALVES["first"]] == 1
    none = [[], []]

    @pl.when(odd)
    def _():
        run(none + two(b_ref) + two(a_ref) + two(one_ref, other_ref))

    @pl.when(jnp.logical_not(odd))
    def _():
        run(two(one_ref, other_ref) + two(a_ref) + two(b_ref) + none)


def move_rows(at, first, second, halo, update, weights):
    rows, cols = update.shape

    def kernel(*refs):
        rows_kernel(64, *refs)

    def whole(array):
        return pl.BlockSpec(array.shape, lambda s, a: (0, 0))

    return pl.pallas_call(
        kernel,
        out_shape=jax.ShapeDtypeStruct((rows, cols), jnp.float32),
        grid_spec=pltpu.PrefetchScalarGridSpec(
            num_scalar_prefetch=1,
            grid=(1,),
            in_specs=[whole(array) for array in (first, second, *halo, update, weights)],
            out_specs=whole(update),
            scratch_shapes=[pltpu.VMEM((rows + 2 * MAPX, cols), jnp.float32)],
        ),
        compiler_params=pltpu.CompilerParams(vmem_limit_bytes=20 << 20),
        cost_estimate=pl.CostEstimate(
            flops=24 * rows * cols, bytes_accessed=16 * rows * cols, transcendentals=0
        ),
        name="move_rows",
    )(at, first, second, *halo, update, weights)


def last_kernel(chunk, at_ref, result_ref, one_ref, other_ref, weights_ref, out_ref, once_ref):
    near, far = [(once_ref, 0)], [(once_ref, MAPX)]

    def into(at):
        def emit(start, value):
            once_ref[pl.ds(at + start, chunk), :] = value

        return emit

    def add(at):
        def emit(start, value):
            rows = pl.ds(at + start, chunk)
            out_ref[rows, :] = result_ref[rows, :] + value

        return emit

    def step(before, here, behind, m, emit):
        step_rows(chunk, before, here, behind, weights_ref, MAPX * (m - 1), emit)

    odd = at_ref[HALVES["first"]] == 1
    halo = two(one_ref, other_ref)

    @pl.when(odd)
    def _():
        step(halo[0], halo[1], [], 1, into(MAPX))
        step(halo[1], [], [], 2, into(0))
        step(far, near, [], 2, add(0))
        step(near, [], [], 3, add(MAPX))

    @pl.when(jnp.logical_not(odd))
    def _():
        step([], halo[0], halo[1], 6, into(MAPX))
        step([], [], halo[0], 5, into(0))
        step([], near, far, 5, add(MAPX))
        step([], [], near, 4, add(0))


def add_last(at, result, halo, weights):
    rows, cols = result.shape
    tile = 256
    block = pl.BlockSpec((rows // 2, tile), lambda s, a: (a[HALVES["second"]], s))
    part = pl.BlockSpec((rows // 2, tile), lambda s, a: (0, s))

    def kernel(*refs):
        last_kernel(64, *refs)

    return pl.pallas_call(
        kernel,
        out_shape=jax.ShapeDtypeStruct(result.shape, result.dtype),
        grid_spec=pltpu.PrefetchScalarGridSpec(
            num_scalar_prefetch=1,
            grid=(cols // tile,),
            in_specs=[block, part, part, pl.BlockSpec(weights.shape, lambda s, a: (0, 0))],
            out_specs=block,
            scratch_shapes=[pltpu.VMEM((2 * MAPX, tile), jnp.float32)],
        ),
        input_output_aliases={1: 0},
        compiler_params=SMALL,
        cost_estimate=pl.CostEstimate(
            flops=10 * rows * cols, bytes_accessed=8 * rows * cols, transcendentals=0
        ),
        name="add_last",
    )(at, result, *halo, weights)


def local(covariance, wind_mask, wind_speed, obs_cells, obs_scale, gain):
    rows, cols = covariance.shape
    row_parts = lax.axis_size("row")
    col_parts = lax.axis_size("col")
    assert row_parts == 16 and rows == 4 * MAPX and cols == 2 * MAPX
    row_at = lax.axis_index("row")
    col_at = lax.axis_index("col")
    near_swap = [(j, j ^ 1) for j in range(col_parts)]
    far_swap = [(j, (j - 1 ^ 1) + 1) for j in range(1, col_parts - 1)]
    turning = [(a, b) for a, b in far_swap if a % 4 in (0, 3)]
    straight = [(a, b) for a, b in far_swap if a % 4 in (1, 2)]
    first, second = row_at % 2, 1 - row_at % 2
    at = jnp.stack([row_at * (rows // MAPX), col_at * (cols // MAPX), row_at])
    turns = jnp.where((col_at % 4 == 0) | (col_at % 4 == 3), 1, 0)
    place = jnp.stack([col_at % 2, first, second, turns])
    half = rows // 2

    def row_swap(odd, kinds):
        cells = [(i, (i - odd ^ 1) + odd) for i in range(odd, row_parts - odd)]
        columns = [j for j in range(col_parts) if j % 4 in kinds]
        return [(a * col_parts + j, b * col_parts + j) for a, b in cells for j in columns]

    def across(bit):
        return [(i, i ^ bit) for i in range(row_parts)]

    far_turning = lax.ppermute(covariance, "col", turning)
    near = lax.ppermute(covariance, "col", near_swap)

    def far_part(number, source):
        block = lax.dynamic_slice_in_dim(source, number * half, half, 0)
        return lax.ppermute(block, "col", straight)


    select, col_weights, down_weights = prepare(
        at, wind_mask, wind_speed, obs_cells, rows, cols, row_parts
    )
    part = jnp.dot(select, covariance, precision=HIGH, preferred_element_type=jnp.float32)

    def sum_over(value, bits):
        size = value.shape[0] // (len(bits) + 1)
        total = value[:size]
        for n, bit in enumerate(bits, 1):
            piece = value[size * n : size * (n + 1)]
            total = total + lax.ppermute(piece, "row", across(bit))
        return total

    def all_of(value, bits):
        return [value] + [lax.ppermute(value, "row", across(bit)) for bit in bits]

    total = sum_over(part, X_BITS)
    total = sum_over(total, Z_BITS)
    each = total.shape[0]

    def move(block, *straight_parts, only=None):
        fars = [(far_turning, block)] + [(part, 0) for part in straight_parts]
        return move_cols(place, (covariance, block), (near, block), fars, col_weights, half, only)

    def swap_rows(block, odd, kinds):
        return lax.ppermute(block, ("row", "col"), row_swap(odd, kinds))

    piece_far = lax.ppermute(total, "col", far_swap)
    far_first = far_part(first, after(covariance, select))
    piece_near = lax.ppermute(total, "col", near_swap)
    piece = move_cols(place, (total, 0), (piece_near, 0), [(piece_far, 0)], col_weights, each)
    observed = all_of(piece, Z_BITS)
    far_second = far_part(second, after(covariance, select))

    early_first = move("first", only="turns")
    halo_first = [swap_rows(early_first, 1, (0, 3))]
    early_second = move("second", only="turns")
    halo_second = [swap_rows(early_second, 0, (0, 3))]

    moved_first = move("first", far_first)
    halo_first.append(swap_rows(moved_first, 1, (1, 2)))

    observed = jnp.concatenate([after(observed[0], moved_first), *observed[1:]])
    observed = jnp.concatenate(all_of(observed, X_BITS))
    index = jnp.arange(gain.shape[1], dtype=jnp.int32)
    reorder = (index[:, None] ^ (row_at * each)) == index[None, :]
    ordered_gain = jnp.dot(gain, reorder.astype(gain.dtype), preferred_element_type=jnp.float32)
    ordered_scale = jnp.sum(jnp.where(reorder, obs_scale[:, None], 0.0), axis=0)
    ordered_gain = ordered_gain * ordered_scale[None, :]
    update = jnp.dot(ordered_gain, observed, precision=HIGH, preferred_element_type=jnp.float32)

    moved_second = move("second", after(far_second, update))
    halo_second.append(swap_rows(moved_second, 0, (1, 2)))

    result = move_rows(place, moved_first, moved_second, halo_first, update, down_weights)
    return add_last(place, result, halo_second, down_weights)


HALVES = {"first": 1, "second": 2, "turns": 3}
X_BITS = (4, 8, 12)
Z_BITS = (1, 2, 3)


def solution(mesh):
    placed = (P("row", "col"), P(), P(), P(), P(), P("row", None))
    return jax.shard_map(
        local, mesh=mesh, in_specs=placed, out_specs=P("row", "col"), check_vma=False
    )
```

```python
import jax
import jax.numpy as jnp
from jax import lax
from jax.experimental import pallas as pl
from jax.experimental.pallas import tpu as pltpu
from jax.sharding import PartitionSpec as P


MAPX = 256
LANE = 128


diffusion = 0.05
HIGH = lax.Precision.HIGHEST
SMALL = pltpu.CompilerParams(vmem_limit_bytes=16 << 20)


def after(value, *earlier):
    return lax.optimization_barrier((value,) + earlier)[0]


def weights_table(map_total, map_row, mask_ref, speed_ref):
    inside = (map_row >= 0) & (map_row < map_total)
    cells = pl.ds(pl.multiple_of(jnp.clip(map_row, 0, map_total - 1) * MAPX, MAPX), MAPX)
    speed = speed_ref[:, cells]
    sign = mask_ref[:, cells].astype(jnp.float32)
    column = lax.broadcasted_iota(jnp.int32, (1, MAPX), 1)
    speed_x, speed_y = speed[0:1], speed[1:2]
    sign_x, sign_y = sign[0:1], sign[1:2]
    middle = 1.0 - speed_x - speed_y - 4.0 * diffusion
    western = jnp.where(column > 0, speed_x * sign_x + diffusion, 0.0)
    eastern = jnp.where(column < MAPX - 1, speed_x * (1.0 - sign_x) + diffusion, 0.0)
    northern = jnp.where(map_row > 0, speed_y * sign_y + diffusion, 0.0)
    southern = jnp.where(map_row < map_total - 1, speed_y * (1.0 - sign_y) + diffusion, 0.0)
    zero = jnp.zeros_like(middle)
    table = jnp.concatenate(
        [middle, western, eastern, northern, southern, zero, zero, zero], axis=0
    )
    return jnp.where(inside, table, 0.0)


def prepare_kernel(rows, map_total, at_ref, mask_ref, speed_ref, *refs):
    cell_refs, (out_ref, cols_ref, down_ref, rows_ref, counts_ref) = refs[:-5], refs[-5:]

    @pl.when(pl.program_id(0) == 0)
    def _():
        last = rows_ref.shape[1] // MAPX - 1
        for m in range(last + 1):
            table = weights_table(map_total, at_ref[0] + m - 2, mask_ref, speed_ref)
            rows_ref[:, MAPX * m : MAPX * (m + 1)] = table
            if 0 < m < last:
                down_ref[MAPX * (m - 1) : MAPX * m, :] = table.T
        for m in range(cols_ref.shape[1] // MAPX):
            cols_ref[:, MAPX * m : MAPX * (m + 1)] = weights_table(
                map_total, at_ref[1] + m - 1, mask_ref, speed_ref
            )

    each = cell_refs[0].shape[0]
    window = rows_ref.shape[1]
    blocks = window // LANE
    block_index = lax.broadcasted_iota(jnp.int32, (blocks, LANE), 0)
    lane_index = lax.broadcasted_iota(jnp.int32, (LANE, LANE), 0)
    for n, cells_ref in enumerate(cell_refs):
        place = cells_ref[...] - (at_ref[2] * rows - 2 * MAPX)
        block_of, lane_of = place >> 7, place & (LANE - 1)
        for o in range(each):
            block_hit = jnp.where(block_of[o : o + 1] == block_index, 1.0, 0.0).astype(jnp.bfloat16)
            lane_hit = jnp.where(lane_of[o : o + 1] == lane_index, 1.0, 0.0).astype(jnp.bfloat16)
            counts_ref[n * each + o] = lax.dot_general(
                block_hit, lane_hit, (((1,), (1,)), ((), ())), preferred_element_type=jnp.float32
            )

    def weights(k, m):
        return rows_ref[k : k + 1, MAPX * m : MAPX * (m + 1)]

    maps = [
        jnp.concatenate([counts_ref[:, 2 * m, :], counts_ref[:, 2 * m + 1, :]], axis=1)
        for m in range(window // MAPX)
    ]
    for first in (0, 1):
        moved = []
        for m in range(1, len(maps) - 1):
            t = m + first
            here = maps[m]
            value = weights(0, t) * here + pltpu.roll(weights(1, t) * here, MAPX - 1, 1)
            value = value + pltpu.roll(weights(2, t) * here, 1, 1)
            value = value + weights(3, t + 1) * maps[m + 1] + weights(4, t - 1) * maps[m - 1]
            moved.append(value)
        maps = moved
    for m, value in enumerate(maps):
        out_ref[:, MAPX * m : MAPX * (m + 1)] = value


def prepare(at, wind_mask, wind_speed, obs_cells, rows, cols, pieces, group=4):
    obs_count, foot = obs_cells.shape
    each = obs_count // pieces
    map_total = wind_speed.shape[1] // MAPX

    def kernel(*refs):
        prepare_kernel(rows, map_total, *refs)

    def fixed(shape):
        return pl.BlockSpec(shape, lambda s, a: (0, 0))

    col_shape = (8, cols + 2 * MAPX)
    down_shape = (rows + 2 * MAPX, 8)
    window = rows + 4 * MAPX
    return pl.pallas_call(
        kernel,
        out_shape=(
            jax.ShapeDtypeStruct((obs_count, rows), jnp.float32),
            jax.ShapeDtypeStruct(col_shape, jnp.float32),
            jax.ShapeDtypeStruct(down_shape, jnp.float32),
        ),
        grid_spec=pltpu.PrefetchScalarGridSpec(
            num_scalar_prefetch=1,
            grid=(pieces // group,),
            in_specs=[fixed(wind_mask.shape), fixed(wind_speed.shape)]
            + [
                pl.BlockSpec((each, foot), lambda s, a, n=n: (s * group + n ^ a[2], 0))
                for n in range(group)
            ],
            out_specs=(
                pl.BlockSpec((each * group, rows), lambda s, a: (s, 0)),
                fixed(col_shape),
                fixed(down_shape),
            ),
            scratch_shapes=[
                pltpu.VMEM((8, window), jnp.float32),
                pltpu.VMEM((each * group, window // LANE, LANE), jnp.float32),
            ],
        ),
        cost_estimate=pl.CostEstimate(flops=1 << 27, bytes_accessed=1 << 21, transcendentals=0),
        name="prepare",
    )(at, wind_mask, wind_speed, *[obs_cells] * group)


def step_cols(before, here, behind, weights):
    width = here.shape[1]
    result = weights[0] * here + weights[1] * pltpu.roll(here, 1, 1)
    result = result + weights[2] * pltpu.roll(here, width - 1, 1)
    return result + weights[3] * before + weights[4] * behind


def cols_kernel(inner, unroll, spans, at_ref, here_ref, near_ref, *refs):
    far_refs, (weights_ref, out_ref) = refs[:-2], refs[-2:]
    step = pl.program_id(0)
    first = at_ref[0] == 0

    def weights(m):
        return [weights_ref[k : k + 1, MAPX * m : MAPX * (m + 1)] for k in range(5)]

    def body(t, carry):
        rows = pl.ds(pl.multiple_of(t * inner, inner), inner)
        near, here = near_ref[rows, :], here_ref[rows, :]
        far = far_refs[0][rows, :]
        for ref, (low, count) in zip(far_refs[1:], spans[1:]):
            far = far + jnp.where((step >= low) & (step < low + count), ref[rows, :], 0.0)
        west = jnp.where(first, far, near)
        east = jnp.where(first, near, far)
        maps = [part[:, MAPX * k : MAPX * (k + 1)] for part in (west, here, east) for k in range(2)]
        once = [step_cols(maps[m], maps[m + 1], maps[m + 2], weights(m)) for m in range(4)]
        for m in range(2):
            out_ref[rows, MAPX * m : MAPX * (m + 1)] = step_cols(
                once[m], once[m + 1], once[m + 2], weights(m + 1)
            )
        return carry

    lax.fori_loop(0, here_ref.shape[0] // inner, body, 0, unroll=unroll)


def move_cols(at, here, near, fars, weights, rows, only=None):
    cols = here[0].shape[1]
    tile = min(rows, 128)
    inner = min(rows, 64)
    steps = rows // tile
    spans, covered = [(0, steps)], 0
    for array, _ in fars[1:]:
        spans.append((covered, array.shape[0] // tile))
        covered += array.shape[0] // tile

    def kernel(at_ref, *refs):
        if only is None:
            cols_kernel(inner, tile // inner, spans, at_ref, *refs)
        else:

            @pl.when(at_ref[HALVES[only]] == 1)
            def _():
                cols_kernel(inner, tile // inner, spans, at_ref, *refs)

    def spec(block):
        def index(s, a):
            at_block = a[HALVES[block]] if isinstance(block, str) else block
            row = at_block * steps + s
            return (row if only is None else row * a[HALVES[only]], 0)

        return pl.BlockSpec((tile, cols), index)

    def part_spec(low, count):
        return pl.BlockSpec((tile, cols), lambda s, a: (jnp.clip(s - low, 0, count - 1), 0))

    blocks = [here, near, fars[0]]
    arrays = [array for array, _ in (here, near, *fars)]
    return pl.pallas_call(
        kernel,
        out_shape=jax.ShapeDtypeStruct((rows, cols), jnp.float32),
        grid_spec=pltpu.PrefetchScalarGridSpec(
            num_scalar_prefetch=1,
            grid=(steps,),
            in_specs=[spec(block) for _, block in blocks]
            + [part_spec(*span) for span in spans[1:]]
            + [pl.BlockSpec(weights.shape, lambda s, a: (0, 0))],
            out_specs=spec(0),
        ),
        compiler_params=SMALL,
        cost_estimate=pl.CostEstimate(
            flops=27 * rows * cols, bytes_accessed=16 * rows * cols, transcendentals=0
        ),
        name="move_cols",
    )(at, *arrays, weights)


def load(parts, start, size):
    value = None
    for ref, base in parts:
        part = ref[pl.ds(base + start, size), :]
        value = part if value is None else value + part
    return value


def step_rows(chunk, before, here, behind, weights_ref, weights_at, emit):
    def body(c, carry):
        start = pl.multiple_of(c * chunk, chunk)
        low = pl.multiple_of(jnp.maximum(start - 8, 0), 8)
        high = pl.multiple_of(jnp.minimum(start + chunk, MAPX - 8), 8)
        weights = weights_ref[pl.ds(weights_at + start, chunk), :]
        terms = []
        if here:
            center = load(here, start, chunk)
            wide = jnp.concatenate([load(here, low, 8), center, load(here, high, 8)], axis=0)
            terms.append(weights[:, 0:1] * center)
            terms.append(weights[:, 1:2] * pltpu.roll(wide, 1, 0)[8 : 8 + chunk])
            terms.append(weights[:, 2:3] * pltpu.roll(wide, chunk + 15, 0)[8 : 8 + chunk])
        if before:
            terms.append(weights[:, 3:4] * load(before, start, chunk))
        if behind:
            terms.append(weights[:, 4:5] * load(behind, start, chunk))
        value = terms[0]
        for term in terms[1:]:
            value = value + term
        emit(start, value)
        return carry

    lax.fori_loop(0, MAPX // chunk, body, 0, unroll=MAPX // chunk)


def two(*refs):
    return [[(ref, MAPX * k) for ref in refs] for k in range(2)]


def rows_kernel(chunk, at_ref, a_ref, b_ref, one_ref, other_ref, update_ref, weights_ref, out_ref, once_ref):
    def run(maps):
        once = {}
        for m in range(1, 7):
            at = MAPX * (m - 1)

            def emit(start, value, at=at):
                once_ref[pl.ds(at + start, chunk), :] = value

            step_rows(chunk, maps[m - 1], maps[m], maps[m + 1], weights_ref, at, emit)
            once[m] = [(once_ref, at)]
        for m in range(2, 6):
            at = MAPX * (m - 2)

            def emit(start, value, at=at):
                rows = pl.ds(at + start, chunk)
                out_ref[rows, :] = value - update_ref[rows, :]

            step_rows(chunk, once[m - 1], once[m], once[m + 1], weights_ref, MAPX * (m - 1), emit)

    odd = at_ref[HALVES["first"]] == 1
    none = [[], []]

    @pl.when(odd)
    def _():
        run(none + two(b_ref) + two(a_ref) + two(one_ref, other_ref))

    @pl.when(jnp.logical_not(odd))
    def _():
        run(two(one_ref, other_ref) + two(a_ref) + two(b_ref) + none)


def move_rows(at, first, second, halo, update, weights):
    rows, cols = update.shape

    def kernel(*refs):
        rows_kernel(64, *refs)

    def whole(array):
        return pl.BlockSpec(array.shape, lambda s, a: (0, 0))

    return pl.pallas_call(
        kernel,
        out_shape=jax.ShapeDtypeStruct((rows, cols), jnp.float32),
        grid_spec=pltpu.PrefetchScalarGridSpec(
            num_scalar_prefetch=1,
            grid=(1,),
            in_specs=[whole(array) for array in (first, second, *halo, update, weights)],
            out_specs=whole(update),
            scratch_shapes=[pltpu.VMEM((rows + 2 * MAPX, cols), jnp.float32)],
        ),
        compiler_params=pltpu.CompilerParams(vmem_limit_bytes=20 << 20),
        cost_estimate=pl.CostEstimate(
            flops=24 * rows * cols, bytes_accessed=16 * rows * cols, transcendentals=0
        ),
        name="move_rows",
    )(at, first, second, *halo, update, weights)


def last_kernel(chunk, at_ref, result_ref, one_ref, other_ref, weights_ref, out_ref, once_ref):
    near, far = [(once_ref, 0)], [(once_ref, MAPX)]

    def into(at):
        def emit(start, value):
            once_ref[pl.ds(at + start, chunk), :] = value

        return emit

    def add(at):
        def emit(start, value):
            rows = pl.ds(at + start, chunk)
            out_ref[rows, :] = result_ref[rows, :] + value

        return emit

    def step(before, here, behind, m, emit):
        step_rows(chunk, before, here, behind, weights_ref, MAPX * (m - 1), emit)

    odd = at_ref[HALVES["first"]] == 1
    halo = two(one_ref, other_ref)

    @pl.when(odd)
    def _():
        step(halo[0], halo[1], [], 1, into(MAPX))
        step(halo[1], [], [], 2, into(0))
        step(far, near, [], 2, add(0))
        step(near, [], [], 3, add(MAPX))

    @pl.when(jnp.logical_not(odd))
    def _():
        step([], halo[0], halo[1], 6, into(MAPX))
        step([], [], halo[0], 5, into(0))
        step([], near, far, 5, add(MAPX))
        step([], [], near, 4, add(0))


def add_last(at, result, halo, weights):
    rows, cols = result.shape
    tile = 256
    block = pl.BlockSpec((rows // 2, tile), lambda s, a: (a[HALVES["second"]], s))
    part = pl.BlockSpec((rows // 2, tile), lambda s, a: (0, s))

    def kernel(*refs):
        last_kernel(64, *refs)

    return pl.pallas_call(
        kernel,
        out_shape=jax.ShapeDtypeStruct(result.shape, result.dtype),
        grid_spec=pltpu.PrefetchScalarGridSpec(
            num_scalar_prefetch=1,
            grid=(cols // tile,),
            in_specs=[block, part, part, pl.BlockSpec(weights.shape, lambda s, a: (0, 0))],
            out_specs=block,
            scratch_shapes=[pltpu.VMEM((2 * MAPX, tile), jnp.float32)],
        ),
        input_output_aliases={1: 0},
        compiler_params=SMALL,
        cost_estimate=pl.CostEstimate(
            flops=10 * rows * cols, bytes_accessed=8 * rows * cols, transcendentals=0
        ),
        name="add_last",
    )(at, result, *halo, weights)


def local(covariance, wind_mask, wind_speed, obs_cells, obs_scale, gain):
    rows, cols = covariance.shape
    row_parts = lax.axis_size("row")
    col_parts = lax.axis_size("col")
    assert row_parts == 16 and rows == 4 * MAPX and cols == 2 * MAPX
    row_at = lax.axis_index("row")
    col_at = lax.axis_index("col")
    near_swap = [(j, j ^ 1) for j in range(col_parts)]
    far_swap = [(j, (j - 1 ^ 1) + 1) for j in range(1, col_parts - 1)]
    turning = [(a, b) for a, b in far_swap if a % 4 in (0, 3)]
    straight = [(a, b) for a, b in far_swap if a % 4 in (1, 2)]
    first, second = row_at % 2, 1 - row_at % 2
    at = jnp.stack([row_at * (rows // MAPX), col_at * (cols // MAPX), row_at])
    turns = jnp.where((col_at % 4 == 0) | (col_at % 4 == 3), 1, 0)
    place = jnp.stack([col_at % 2, first, second, turns])
    half = rows // 2

    def row_swap(odd, kinds):
        cells = [(i, (i - odd ^ 1) + odd) for i in range(odd, row_parts - odd)]
        columns = [j for j in range(col_parts) if j % 4 in kinds]
        return [(a * col_parts + j, b * col_parts + j) for a, b in cells for j in columns]

    def across(bit):
        return [(i, i ^ bit) for i in range(row_parts)]

    far_turning = lax.ppermute(covariance, "col", turning)
    near = lax.ppermute(covariance, "col", near_swap)

    def far_part(start, size, source):
        block = lax.dynamic_slice_in_dim(source, start, size, 0)
        return lax.ppermute(block, "col", straight)

    far_begin = far_part(first * half, MAPX, covariance)


    select, col_weights, down_weights = prepare(
        at, wind_mask, wind_speed, obs_cells, rows, cols, row_parts
    )
    part = jnp.dot(select, covariance, precision=HIGH, preferred_element_type=jnp.float32)

    def sum_over(value, bits):
        size = value.shape[0] // (len(bits) + 1)
        total = value[:size]
        for n, bit in enumerate(bits, 1):
            piece = value[size * n : size * (n + 1)]
            total = total + lax.ppermute(piece, "row", across(bit))
        return total

    def all_of(value, bits):
        return [value] + [lax.ppermute(value, "row", across(bit)) for bit in bits]

    total = sum_over(part, X_BITS)
    total = sum_over(total, Z_BITS)
    each = total.shape[0]

    def move(block, *straight_parts, only=None):
        fars = [(far_turning, block)] + [(part, 0) for part in straight_parts]
        return move_cols(place, (covariance, block), (near, block), fars, col_weights, half, only)

    def swap_rows(block, odd, kinds):
        return lax.ppermute(block, ("row", "col"), row_swap(odd, kinds))

    piece_far = lax.ppermute(total, "col", far_swap)
    late = after(covariance, select)
    far_first = far_part(first * half + MAPX, half - MAPX, late)

    early_first = move("first", only="turns")
    early_second = move("second", only="turns")
    piece_near = lax.ppermute(total, "col", near_swap)
    piece = move_cols(place, (total, 0), (piece_near, 0), [(piece_far, 0)], col_weights, each)
    observed = all_of(piece, Z_BITS)
    halo_first = [swap_rows(early_first, 1, (0, 3))]
    halo_second = [swap_rows(early_second, 0, (0, 3))]
    far_second = far_part(second * half, half, late)

    moved_first = move("first", far_begin, far_first)
    halo_first.append(swap_rows(moved_first, 1, (1, 2)))

    observed = jnp.concatenate([after(observed[0], moved_first), *observed[1:]])
    observed = jnp.concatenate(all_of(observed, X_BITS))
    index = jnp.arange(gain.shape[1], dtype=jnp.int32)
    reorder = (index[:, None] ^ (row_at * each)) == index[None, :]
    ordered_gain = jnp.dot(gain, reorder.astype(gain.dtype), preferred_element_type=jnp.float32)
    ordered_scale = jnp.sum(jnp.where(reorder, obs_scale[:, None], 0.0), axis=0)
    ordered_gain = ordered_gain * ordered_scale[None, :]
    update = jnp.dot(ordered_gain, observed, precision=HIGH, preferred_element_type=jnp.float32)

    moved_second = move("second", after(far_second, update))
    halo_second.append(swap_rows(moved_second, 0, (1, 2)))

    result = move_rows(place, moved_first, moved_second, halo_first, update, down_weights)
    return add_last(place, result, halo_second, down_weights)


HALVES = {"first": 1, "second": 2, "turns": 3}
X_BITS = (4, 8, 12)
Z_BITS = (1, 2, 3)


def solution(mesh):
    placed = (P("row", "col"), P(), P(), P(), P(), P("row", None))
    return jax.shard_map(
        local, mesh=mesh, in_specs=placed, out_specs=P("row", "col"), check_vma=False
    )
```

```python
import jax
import jax.numpy as jnp
from jax import lax
from jax.experimental import pallas as pl
from jax.experimental.pallas import tpu as pltpu
from jax.sharding import PartitionSpec as P


MAPX = 256
LANE = 128


diffusion = 0.05
HIGH = lax.Precision.HIGHEST
SMALL = pltpu.CompilerParams(vmem_limit_bytes=16 << 20)


def after(value, *earlier):
    return lax.optimization_barrier((value,) + earlier)[0]


def weights_table(map_total, map_row, mask_ref, speed_ref):
    inside = (map_row >= 0) & (map_row < map_total)
    cells = pl.ds(pl.multiple_of(jnp.clip(map_row, 0, map_total - 1) * MAPX, MAPX), MAPX)
    speed = speed_ref[:, cells]
    sign = mask_ref[:, cells].astype(jnp.float32)
    column = lax.broadcasted_iota(jnp.int32, (1, MAPX), 1)
    speed_x, speed_y = speed[0:1], speed[1:2]
    sign_x, sign_y = sign[0:1], sign[1:2]
    middle = 1.0 - speed_x - speed_y - 4.0 * diffusion
    western = jnp.where(column > 0, speed_x * sign_x + diffusion, 0.0)
    eastern = jnp.where(column < MAPX - 1, speed_x * (1.0 - sign_x) + diffusion, 0.0)
    northern = jnp.where(map_row > 0, speed_y * sign_y + diffusion, 0.0)
    southern = jnp.where(map_row < map_total - 1, speed_y * (1.0 - sign_y) + diffusion, 0.0)
    zero = jnp.zeros_like(middle)
    table = jnp.concatenate(
        [middle, western, eastern, northern, southern, zero, zero, zero], axis=0
    )
    return jnp.where(inside, table, 0.0)


def prepare_kernel(rows, map_total, at_ref, mask_ref, speed_ref, *refs):
    cell_refs, (out_ref, cols_ref, down_ref, rows_ref, counts_ref) = refs[:-5], refs[-5:]

    @pl.when(pl.program_id(0) == 0)
    def _():
        last = rows_ref.shape[1] // MAPX - 1
        for m in range(last + 1):
            table = weights_table(map_total, at_ref[0] + m - 2, mask_ref, speed_ref)
            rows_ref[:, MAPX * m : MAPX * (m + 1)] = table
            if 0 < m < last:
                down_ref[MAPX * (m - 1) : MAPX * m, :] = table.T
        for m in range(cols_ref.shape[1] // MAPX):
            cols_ref[:, MAPX * m : MAPX * (m + 1)] = weights_table(
                map_total, at_ref[1] + m - 1, mask_ref, speed_ref
            )

    each = cell_refs[0].shape[0]
    window = rows_ref.shape[1]
    blocks = window // LANE
    block_index = lax.broadcasted_iota(jnp.int32, (blocks, LANE), 0)
    lane_index = lax.broadcasted_iota(jnp.int32, (LANE, LANE), 0)
    for n, cells_ref in enumerate(cell_refs):
        place = cells_ref[...] - (at_ref[2] * rows - 2 * MAPX)
        block_of, lane_of = place >> 7, place & (LANE - 1)
        for o in range(each):
            block_hit = jnp.where(block_of[o : o + 1] == block_index, 1.0, 0.0).astype(jnp.bfloat16)
            lane_hit = jnp.where(lane_of[o : o + 1] == lane_index, 1.0, 0.0).astype(jnp.bfloat16)
            counts_ref[n * each + o] = lax.dot_general(
                block_hit, lane_hit, (((1,), (1,)), ((), ())), preferred_element_type=jnp.float32
            )

    def weights(k, m):
        return rows_ref[k : k + 1, MAPX * m : MAPX * (m + 1)]

    maps = [
        jnp.concatenate([counts_ref[:, 2 * m, :], counts_ref[:, 2 * m + 1, :]], axis=1)
        for m in range(window // MAPX)
    ]
    for first in (0, 1):
        moved = []
        for m in range(1, len(maps) - 1):
            t = m + first
            here = maps[m]
            value = weights(0, t) * here + pltpu.roll(weights(1, t) * here, MAPX - 1, 1)
            value = value + pltpu.roll(weights(2, t) * here, 1, 1)
            value = value + weights(3, t + 1) * maps[m + 1] + weights(4, t - 1) * maps[m - 1]
            moved.append(value)
        maps = moved
    for m, value in enumerate(maps):
        out_ref[:, MAPX * m : MAPX * (m + 1)] = value


def prepare(at, wind_mask, wind_speed, obs_cells, rows, cols, pieces, group=4):
    obs_count, foot = obs_cells.shape
    each = obs_count // pieces
    map_total = wind_speed.shape[1] // MAPX

    def kernel(*refs):
        prepare_kernel(rows, map_total, *refs)

    def fixed(shape):
        return pl.BlockSpec(shape, lambda s, a: (0, 0))

    col_shape = (8, cols + 2 * MAPX)
    down_shape = (rows + 2 * MAPX, 8)
    window = rows + 4 * MAPX
    return pl.pallas_call(
        kernel,
        out_shape=(
            jax.ShapeDtypeStruct((obs_count, rows), jnp.float32),
            jax.ShapeDtypeStruct(col_shape, jnp.float32),
            jax.ShapeDtypeStruct(down_shape, jnp.float32),
        ),
        grid_spec=pltpu.PrefetchScalarGridSpec(
            num_scalar_prefetch=1,
            grid=(pieces // group,),
            in_specs=[fixed(wind_mask.shape), fixed(wind_speed.shape)]
            + [
                pl.BlockSpec((each, foot), lambda s, a, n=n: (s * group + n ^ a[2], 0))
                for n in range(group)
            ],
            out_specs=(
                pl.BlockSpec((each * group, rows), lambda s, a: (s, 0)),
                fixed(col_shape),
                fixed(down_shape),
            ),
            scratch_shapes=[
                pltpu.VMEM((8, window), jnp.float32),
                pltpu.VMEM((each * group, window // LANE, LANE), jnp.float32),
            ],
        ),
        cost_estimate=pl.CostEstimate(flops=1 << 27, bytes_accessed=1 << 21, transcendentals=0),
        name="prepare",
    )(at, wind_mask, wind_speed, *[obs_cells] * group)


def step_cols(before, here, behind, weights):
    width = here.shape[1]
    result = weights[0] * here + weights[1] * pltpu.roll(here, 1, 1)
    result = result + weights[2] * pltpu.roll(here, width - 1, 1)
    return result + weights[3] * before + weights[4] * behind


def cols_kernel(inner, unroll, spans, at_ref, here_ref, near_ref, *refs):
    far_refs, (weights_ref, out_ref) = refs[:-2], refs[-2:]
    step = pl.program_id(0)
    first = at_ref[0] == 0

    def weights(m):
        return [weights_ref[k : k + 1, MAPX * m : MAPX * (m + 1)] for k in range(5)]

    def body(t, carry):
        rows = pl.ds(pl.multiple_of(t * inner, inner), inner)
        near, here = near_ref[rows, :], here_ref[rows, :]
        far = far_refs[0][rows, :]
        for ref, (low, count) in zip(far_refs[1:], spans[1:]):
            far = far + jnp.where((step >= low) & (step < low + count), ref[rows, :], 0.0)
        west = jnp.where(first, far, near)
        east = jnp.where(first, near, far)
        maps = [part[:, MAPX * k : MAPX * (k + 1)] for part in (west, here, east) for k in range(2)]
        once = [step_cols(maps[m], maps[m + 1], maps[m + 2], weights(m)) for m in range(4)]
        for m in range(2):
            out_ref[rows, MAPX * m : MAPX * (m + 1)] = step_cols(
                once[m], once[m + 1], once[m + 2], weights(m + 1)
            )
        return carry

    lax.fori_loop(0, here_ref.shape[0] // inner, body, 0, unroll=unroll)


def move_cols(at, here, near, fars, weights, rows, only=None):
    cols = here[0].shape[1]
    tile = min(rows, 128)
    inner = min(rows, 64)
    steps = rows // tile
    spans, covered = [(0, steps)], 0
    for array, _ in fars[1:]:
        spans.append((covered, array.shape[0] // tile))
        covered += array.shape[0] // tile

    def kernel(at_ref, *refs):
        if only is None:
            cols_kernel(inner, tile // inner, spans, at_ref, *refs)
        else:

            @pl.when(at_ref[HALVES[only]] == 1)
            def _():
                cols_kernel(inner, tile // inner, spans, at_ref, *refs)

    def spec(block):
        def index(s, a):
            at_block = a[HALVES[block]] if isinstance(block, str) else block
            row = at_block * steps + s
            return (row if only is None else row * a[HALVES[only]], 0)

        return pl.BlockSpec((tile, cols), index)

    def part_spec(low, count):
        return pl.BlockSpec((tile, cols), lambda s, a: (jnp.clip(s - low, 0, count - 1), 0))

    blocks = [here, near, fars[0]]
    arrays = [array for array, _ in (here, near, *fars)]
    return pl.pallas_call(
        kernel,
        out_shape=jax.ShapeDtypeStruct((rows, cols), jnp.float32),
        grid_spec=pltpu.PrefetchScalarGridSpec(
            num_scalar_prefetch=1,
            grid=(steps,),
            in_specs=[spec(block) for _, block in blocks]
            + [part_spec(*span) for span in spans[1:]]
            + [pl.BlockSpec(weights.shape, lambda s, a: (0, 0))],
            out_specs=spec(0),
        ),
        compiler_params=SMALL,
        cost_estimate=pl.CostEstimate(
            flops=27 * rows * cols, bytes_accessed=16 * rows * cols, transcendentals=0
        ),
        name="move_cols",
    )(at, *arrays, weights)


def load(parts, start, size):
    value = None
    for ref, base in parts:
        part = ref[pl.ds(base + start, size), :]
        value = part if value is None else value + part
    return value


def step_rows(chunk, before, here, behind, weights_ref, weights_at, emit):
    def body(c, carry):
        start = pl.multiple_of(c * chunk, chunk)
        low = pl.multiple_of(jnp.maximum(start - 8, 0), 8)
        high = pl.multiple_of(jnp.minimum(start + chunk, MAPX - 8), 8)
        weights = weights_ref[pl.ds(weights_at + start, chunk), :]
        terms = []
        if here:
            center = load(here, start, chunk)
            wide = jnp.concatenate([load(here, low, 8), center, load(here, high, 8)], axis=0)
            terms.append(weights[:, 0:1] * center)
            terms.append(weights[:, 1:2] * pltpu.roll(wide, 1, 0)[8 : 8 + chunk])
            terms.append(weights[:, 2:3] * pltpu.roll(wide, chunk + 15, 0)[8 : 8 + chunk])
        if before:
            terms.append(weights[:, 3:4] * load(before, start, chunk))
        if behind:
            terms.append(weights[:, 4:5] * load(behind, start, chunk))
        value = terms[0]
        for term in terms[1:]:
            value = value + term
        emit(start, value)
        return carry

    lax.fori_loop(0, MAPX // chunk, body, 0, unroll=MAPX // chunk)


def two(*refs):
    return [[(ref, MAPX * k) for ref in refs] for k in range(2)]


def rows_kernel(chunk, at_ref, a_ref, b_ref, one_ref, other_ref, update_ref, weights_ref, out_ref, once_ref):
    def run(maps):
        once = {}
        for m in range(1, 7):
            at = MAPX * (m - 1)

            def emit(start, value, at=at):
                once_ref[pl.ds(at + start, chunk), :] = value

            step_rows(chunk, maps[m - 1], maps[m], maps[m + 1], weights_ref, at, emit)
            once[m] = [(once_ref, at)]
        for m in range(2, 6):
            at = MAPX * (m - 2)

            def emit(start, value, at=at):
                rows = pl.ds(at + start, chunk)
                out_ref[rows, :] = value - update_ref[rows, :]

            step_rows(chunk, once[m - 1], once[m], once[m + 1], weights_ref, MAPX * (m - 1), emit)

    odd = at_ref[HALVES["first"]] == 1
    none = [[], []]

    @pl.when(odd)
    def _():
        run(none + two(b_ref) + two(a_ref) + two(one_ref, other_ref))

    @pl.when(jnp.logical_not(odd))
    def _():
        run(two(one_ref, other_ref) + two(a_ref) + two(b_ref) + none)


def move_rows(at, first, second, halo, update, weights):
    rows, cols = update.shape

    def kernel(*refs):
        rows_kernel(64, *refs)

    def whole(array):
        return pl.BlockSpec(array.shape, lambda s, a: (0, 0))

    return pl.pallas_call(
        kernel,
        out_shape=jax.ShapeDtypeStruct((rows, cols), jnp.float32),
        grid_spec=pltpu.PrefetchScalarGridSpec(
            num_scalar_prefetch=1,
            grid=(1,),
            in_specs=[whole(array) for array in (first, second, *halo, update, weights)],
            out_specs=whole(update),
            scratch_shapes=[pltpu.VMEM((rows + 2 * MAPX, cols), jnp.float32)],
        ),
        compiler_params=pltpu.CompilerParams(vmem_limit_bytes=20 << 20),
        cost_estimate=pl.CostEstimate(
            flops=24 * rows * cols, bytes_accessed=16 * rows * cols, transcendentals=0
        ),
        name="move_rows",
    )(at, first, second, *halo, update, weights)


def last_kernel(chunk, at_ref, result_ref, one_ref, other_ref, weights_ref, out_ref, once_ref):
    near, far = [(once_ref, 0)], [(once_ref, MAPX)]

    def into(at):
        def emit(start, value):
            once_ref[pl.ds(at + start, chunk), :] = value

        return emit

    def add(at):
        def emit(start, value):
            rows = pl.ds(at + start, chunk)
            out_ref[rows, :] = result_ref[rows, :] + value

        return emit

    def step(before, here, behind, m, emit):
        step_rows(chunk, before, here, behind, weights_ref, MAPX * (m - 1), emit)

    odd = at_ref[HALVES["first"]] == 1
    halo = two(one_ref, other_ref)

    @pl.when(odd)
    def _():
        step(halo[0], halo[1], [], 1, into(MAPX))
        step(halo[1], [], [], 2, into(0))
        step(far, near, [], 2, add(0))
        step(near, [], [], 3, add(MAPX))

    @pl.when(jnp.logical_not(odd))
    def _():
        step([], halo[0], halo[1], 6, into(MAPX))
        step([], [], halo[0], 5, into(0))
        step([], near, far, 5, add(MAPX))
        step([], [], near, 4, add(0))


def add_last(at, result, halo, weights):
    rows, cols = result.shape
    tile = 256
    block = pl.BlockSpec((rows // 2, tile), lambda s, a: (a[HALVES["second"]], s))
    part = pl.BlockSpec((rows // 2, tile), lambda s, a: (0, s))

    def kernel(*refs):
        last_kernel(64, *refs)

    return pl.pallas_call(
        kernel,
        out_shape=jax.ShapeDtypeStruct(result.shape, result.dtype),
        grid_spec=pltpu.PrefetchScalarGridSpec(
            num_scalar_prefetch=1,
            grid=(cols // tile,),
            in_specs=[block, part, part, pl.BlockSpec(weights.shape, lambda s, a: (0, 0))],
            out_specs=block,
            scratch_shapes=[pltpu.VMEM((2 * MAPX, tile), jnp.float32)],
        ),
        input_output_aliases={1: 0},
        compiler_params=SMALL,
        cost_estimate=pl.CostEstimate(
            flops=10 * rows * cols, bytes_accessed=8 * rows * cols, transcendentals=0
        ),
        name="add_last",
    )(at, result, *halo, weights)


def local(covariance, wind_mask, wind_speed, obs_cells, obs_scale, gain):
    rows, cols = covariance.shape
    row_parts = lax.axis_size("row")
    col_parts = lax.axis_size("col")
    assert row_parts == 16 and rows == 4 * MAPX and cols == 2 * MAPX
    row_at = lax.axis_index("row")
    col_at = lax.axis_index("col")
    near_swap = [(j, j ^ 1) for j in range(col_parts)]
    far_swap = [(j, (j - 1 ^ 1) + 1) for j in range(1, col_parts - 1)]
    turning = [(a, b) for a, b in far_swap if a % 4 in (0, 3)]
    straight = [(a, b) for a, b in far_swap if a % 4 in (1, 2)]
    first, second = row_at % 2, 1 - row_at % 2
    at = jnp.stack([row_at * (rows // MAPX), col_at * (cols // MAPX), row_at])
    turns = jnp.where((col_at % 4 == 0) | (col_at % 4 == 3), 1, 0)
    place = jnp.stack([col_at % 2, first, second, turns])
    half = rows // 2

    def row_swap(odd, kinds):
        cells = [(i, (i - odd ^ 1) + odd) for i in range(odd, row_parts - odd)]
        columns = [j for j in range(col_parts) if j % 4 in kinds]
        return [(a * col_parts + j, b * col_parts + j) for a, b in cells for j in columns]

    def across(bit):
        return [(i, i ^ bit) for i in range(row_parts)]

    far_turning = lax.ppermute(covariance, "col", turning)
    near = lax.ppermute(covariance, "col", near_swap)

    def far_part(start, size, source):
        block = lax.dynamic_slice_in_dim(source, start, size, 0)
        return lax.ppermute(block, "col", straight)

    far_begin = far_part(first * half, MAPX, covariance)


    select, col_weights, down_weights = prepare(
        at, wind_mask, wind_speed, obs_cells, rows, cols, row_parts
    )
    part = jnp.dot(select, covariance, precision=HIGH, preferred_element_type=jnp.float32)

    def sum_over(value, bits):
        size = value.shape[0] // (len(bits) + 1)
        total = value[:size]
        for n, bit in enumerate(bits, 1):
            piece = value[size * n : size * (n + 1)]
            total = total + lax.ppermute(piece, "row", across(bit))
        return total

    def all_of(value, bits):
        return [value] + [lax.ppermute(value, "row", across(bit)) for bit in bits]

    total = sum_over(part, X_BITS)
    total = sum_over(total, Z_BITS)
    each = total.shape[0]

    def move(block, *straight_parts, only=None):
        fars = [(far_turning, block)] + [(part, 0) for part in straight_parts]
        return move_cols(place, (covariance, block), (near, block), fars, col_weights, half, only)

    def swap_rows(block, odd, kinds):
        return lax.ppermute(block, ("row", "col"), row_swap(odd, kinds))

    piece_far = lax.ppermute(total, "col", far_swap)
    late = after(covariance, select)
    far_first = far_part(first * half + MAPX, half - MAPX, late)

    early_first = move("first", only="turns")
    early_second = move("second", only="turns")
    piece_near = lax.ppermute(total, "col", near_swap)
    piece = move_cols(place, (total, 0), (piece_near, 0), [(piece_far, 0)], col_weights, each)
    observed = all_of(piece, Z_BITS)
    halo_first = [swap_rows(early_first, 1, (0, 3))]
    far_second = far_part(second * half, half, late)

    moved_first = move("first", far_begin, far_first)
    halo_first.append(swap_rows(moved_first, 1, (1, 2)))

    moved_second = move("second", far_second)
    halo_second = [swap_rows(moved_second, 0, (1, 2))]

    observed = jnp.concatenate([after(observed[0], moved_second), *observed[1:]])
    observed = jnp.concatenate(all_of(observed, X_BITS))
    index = jnp.arange(gain.shape[1], dtype=jnp.int32)
    reorder = (index[:, None] ^ (row_at * each)) == index[None, :]
    ordered_gain = jnp.dot(gain, reorder.astype(gain.dtype), preferred_element_type=jnp.float32)
    ordered_scale = jnp.sum(jnp.where(reorder, obs_scale[:, None], 0.0), axis=0)
    ordered_gain = ordered_gain * ordered_scale[None, :]
    update = jnp.dot(ordered_gain, observed, precision=HIGH, preferred_element_type=jnp.float32)

    halo_second.append(swap_rows(early_second, 0, (0, 3)))

    result = move_rows(place, moved_first, moved_second, halo_first, update, down_weights)
    return add_last(place, result, halo_second, down_weights)


HALVES = {"first": 1, "second": 2, "turns": 3}
X_BITS = (4, 8, 12)
Z_BITS = (1, 2, 3)


def solution(mesh):
    placed = (P("row", "col"), P(), P(), P(), P(), P("row", None))
    return jax.shard_map(
        local, mesh=mesh, in_specs=placed, out_specs=P("row", "col"), check_vma=False
    )
```
